32 devices in a mesh: groups: 2 (over x), ctx: 16 (over z, y, core).
Axes of the slice: x: 2, y: 2, z: 4, core: 2. Of those that a mesh axis runs over, the one named last changes fastest.
Arguments:
- key_cache: bfloat16 [4, 16384, 128], P(None, ('groups', 'ctx')), parts along dimension 1, may hold values from -16 to 16
- value_cache: bfloat16 [4, 16384, 128], P(None, ('groups', 'ctx')), parts along dimension 1, may hold values from -6 to 6
- init_centroids: bfloat16 [4, 1024, 128], replicated, may hold values from -6 to 6
- block_clusters: int32 [4, 128], P(None, 'groups'), parts along dimension 1, may hold values from 0 to 1023, as said below
- chosen_clusters: int32 [16, 4, 32], P('groups'), parts along dimension 0, may hold values from 0 to 1023, as said below
- request_positions: int32 [16], P('groups'), parts along dimension 0, may hold values from 1 to 8192, as said below
- queries: bfloat16 [16, 4, 8, 128], P('groups'), parts along dimension 0, may hold values from -640 to 640
Outputs:
- centroids: float32 [4, 2048, 128], P(None, ('groups', 'ctx')), parts along dimension 1
- attended: bfloat16 [16, 4, 8, 128], P('groups'), parts along dimension 0
The draws below stay inside these ranges and needn't reach their ends.
There are 2 independent parts, one for each index of `groups`. The reference program is written for one: setup_inputs(seed, part) draws one part's arguments, and reference() takes and returns one part's arrays. A program takes and returns all parts, laid end to end along the dimension named above; an argument that names none is the same for every part. Nothing has to cross between parts.
Inputs may be any that keep to these rules, and one draw needn't show every extreme that they name: `block_clusters`: the owner of cluster c is the ctx index c // 64. Over the 4 x 4 pairs (head, block) of one device's blocks, at most 2 pairs have clusters of one owner; 2 owners get exactly 2 pairs from every device. `chosen_clusters`: the 32 clusters of one request and head are distinct. `request_positions`: at least half of the requests see all 8192 tokens.
All inputs are finite; a program needn't handle non-finite values.
Results may differ from the reference program's by a relative error of at most 0.0078.
Values may be sent and summed in bfloat16 or wider, within the bound.
A program may use at most 64 MiB of HBM per device.

```python
import math
import jax
import jax.numpy as jnp
from jax import lax

DH = 128
HEADS = 4
GROUP = 8
CLUSTERS = 1024
KSEL = 32
BLOCK = 128
REQUESTS = 8
TOK_DEV = 512
TOKENS = 8192
BLK_DEV = 4
NBLK = 64
PER_OWNER = 64
SLOTS = 2
HOT = 2


def shard_directions(key):
    shards = TOKENS // TOK_DEV
    direction = jax.random.normal(jax.random.fold_in(key, 32), (HEADS, shards, DH), jnp.float32)
    return direction / jnp.sqrt(jnp.sum(direction * direction, axis=2, keepdims=True))


def draw_key_cache(key, part):
    shards = TOKENS // TOK_DEV
    noise = jnp.clip(jax.random.normal(jax.random.fold_in(key, 31), (HEADS, TOKENS, DH), jnp.float32), -6.0, 6.0)
    direction = shard_directions(key)
    strength = jnp.ones((HEADS, shards, 1), jnp.float32) * 1.5
    common = jnp.repeat(direction * strength * math.sqrt(DH), TOK_DEV, axis=1)
    return jnp.clip(noise + common, -16.0, 16.0).astype(jnp.bfloat16)


def cluster_table(key):
    senders = NBLK // BLK_DEV
    entries = HEADS * BLK_DEV
    options = senders * SLOTS
    hot_order = jax.random.permutation(jax.random.fold_in(key, 11), senders)
    hot_rank = jnp.zeros((senders,), jnp.int32).at[hot_order].set(jnp.arange(senders, dtype=jnp.int32))
    is_hot = (hot_rank < HOT).astype(jnp.int32)
    slot_owner = jnp.arange(options, dtype=jnp.int32) // SLOTS

    def one_sender(sender):
        sender_key = jax.random.fold_in(jax.random.fold_in(key, 23), sender)
        noise = jax.random.randint(jax.random.fold_in(sender_key, 1), (options,), 0, 65536)
        ranking = is_hot[slot_owner] * 16777216 + noise * options + jnp.arange(options, dtype=jnp.int32)
        _, picked = lax.top_k(ranking, entries)
        shuffled = jax.random.permutation(jax.random.fold_in(sender_key, 2), picked)
        owners = slot_owner[shuffled]
        within = jax.random.randint(jax.random.fold_in(sender_key, 3), (entries,), 0, PER_OWNER)
        return (owners * PER_OWNER + within).reshape(HEADS, BLK_DEV)
    table = jax.vmap(one_sender)(jnp.arange(senders, dtype=jnp.int32))
    return jnp.transpose(table, (1, 0, 2)).reshape(HEADS, NBLK).astype(jnp.int32)


def draw_block_clusters(key, part):
    return cluster_table(key)


def request_plan(key):
    shards = TOKENS // TOK_DEV
    order = jax.random.permutation(jax.random.fold_in(key, 41), REQUESTS)
    ranks = jnp.zeros((REQUESTS,), jnp.int32).at[order].set(jnp.arange(REQUESTS, dtype=jnp.int32))
    full = ranks < REQUESTS // 2
    shard_order = jax.random.permutation(jax.random.fold_in(key, 42), shards).astype(jnp.int32)
    place = ranks[:, None, None] * (HEADS * GROUP) + jnp.arange(HEADS, dtype=jnp.int32)[None, :, None] * GROUP + jnp.arange(GROUP, dtype=jnp.int32)[None, None, :]
    target_shard = shard_order[place % shards]
    target_block = target_shard * BLK_DEV + jax.random.randint(jax.random.fold_in(key, 43), (REQUESTS, HEADS, GROUP), 0, BLK_DEV)
    return (ranks, full, target_shard, target_block.astype(jnp.int32))


def draw_request_positions(key, part):
    ranks, full, target_shard, target_block = request_plan(key)
    drawn = jax.random.randint(jax.random.fold_in(key, 44), (REQUESTS,), 1, TOKENS + 1)
    return jnp.where(full, TOKENS, drawn).astype(jnp.int32)


def draw_chosen_clusters(key, part):
    ranks, full, target_shard, target_block = request_plan(key)
    table = cluster_table(key)
    head_ids = jnp.arange(HEADS, dtype=jnp.int32)
    target_clusters = table[head_ids[None, :, None], target_block]
    cluster_ids = jnp.arange(CLUSTERS, dtype=jnp.int32)
    marked = jnp.any(target_clusters[..., None] == cluster_ids[None, None, None, :], axis=2) & full[:, None, None]
    extra = (ranks == REQUESTS // 2)[:, None, None] & (head_ids == 0)[None, :, None] & ((cluster_ids == 0) | (cluster_ids == CLUSTERS - 1))[None, None, :]
    marked = marked | extra
    noise = jax.random.randint(jax.random.fold_in(key, 45), (REQUESTS, HEADS, CLUSTERS), 0, 1024)
    ranking = marked.astype(jnp.int32) * 4194304 + noise * CLUSTERS + cluster_ids[None, None, :]
    _, picked = lax.top_k(ranking, KSEL)
    return picked.astype(jnp.int32)


def draw_queries(key, part):
    shape = (REQUESTS, HEADS, GROUP, DH)
    ranks, full, target_shard, target_block = request_plan(key)
    direction = shard_directions(key)
    head_ids = jnp.arange(HEADS, dtype=jnp.int32)
    aim = direction[head_ids[None, :, None], target_shard]
    reach = jax.random.uniform(jax.random.fold_in(key, 8), (REQUESTS, HEADS, GROUP, 1), minval=1.5, maxval=3.0)
    aligned = jnp.where(full[:, None, None, None], reach * math.sqrt(DH) * aim, 0.0)
    values_drawn = jnp.clip(jax.random.normal(jax.random.fold_in(key, 5), shape, jnp.float32), -6.0, 6.0)
    values_drawn = jnp.clip(values_drawn + aligned, -8.0, 8.0)
    order = jax.random.permutation(jax.random.fold_in(key, 6), REQUESTS)
    strong_rank = jnp.zeros((REQUESTS,), jnp.int32).at[order].set(jnp.arange(REQUESTS, dtype=jnp.int32))
    strong = (strong_rank < max(1, REQUESTS // 4)).reshape(REQUESTS, 1, 1, 1)
    factor = jnp.exp(jax.random.uniform(jax.random.fold_in(key, 7), (REQUESTS, 1, 1, 1), minval=math.log(40.0), maxval=math.log(80.0)))
    values_drawn = values_drawn * jnp.where(strong, factor, 1.0)
    return values_drawn.astype(jnp.bfloat16)


def shard_levels(own_key, extent, split, low, high):
    loudness, own = 1.0, jax.random.fold_in(own_key, 6)
    for dim, blocks in split:
        steps = jnp.exp(jax.random.uniform(jax.random.fold_in(own, dim), (blocks,), jnp.float32, low / len(split), high / len(split)))
        loudness = loudness * jnp.repeat(steps, extent[dim] // blocks).reshape([-1 if axis == dim else 1 for axis in range(len(extent))])
    return loudness


def normal_values(key, extent, scale, most, split=(), held_as=jnp.bfloat16):
    level = shard_levels(key, extent, split, -0.22, 0.18) if split else 1.0
    values = jax.random.normal(key, extent, jnp.float32) * scale * level
    return jnp.minimum(jnp.maximum(values, -most), most).astype(held_as)


def setup_inputs(seed: int = 0, part: int = 0) -> dict:
    streams_of = jax.random.split(jax.random.key(seed), 8)
    part_splits = jax.random.split(jax.random.fold_in(streams_of[7], part), 8)
    key_cache = draw_key_cache(jax.random.fold_in(jax.random.fold_in(streams_of[7], part), 71), part)
    value_cache = normal_values(part_splits[1], (HEADS, TOKENS, DH), 1.0, 6.0, ((1, 16),))
    init_centroids = normal_values(streams_of[2], (HEADS, CLUSTERS, DH), 1.0, 6.0)
    block_clusters = draw_block_clusters(jax.random.fold_in(jax.random.fold_in(streams_of[7], part), 71), part)
    chosen_clusters = draw_chosen_clusters(jax.random.fold_in(jax.random.fold_in(streams_of[7], part), 71), part)
    request_positions = draw_request_positions(jax.random.fold_in(jax.random.fold_in(streams_of[7], part), 71), part)
    queries = draw_queries(jax.random.fold_in(jax.random.fold_in(streams_of[7], part), 71), part)
    return dict(key_cache=key_cache, value_cache=value_cache, init_centroids=init_centroids, block_clusters=block_clusters, chosen_clusters=chosen_clusters, request_positions=request_positions, queries=queries)


SHARPNESS = 16.0
EPSILON = 1e-06
NEGATIVE = -1e+30

def to_unit(vectors):
    vectors = vectors.astype(jnp.float32)
    return vectors * lax.rsqrt(lax.optimization_barrier(jnp.mean(vectors * vectors, axis=-1, keepdims=True)) + EPSILON) * vectors.shape[-1] ** (-0.5)

def head_sums(keys_head, values_head, cents_head, with_values):
    token_count = keys_head.shape[0]
    block_rows = math.gcd(8192, token_count)
    turn_count = token_count // block_rows
    cluster_count = cents_head.shape[0]
    head_dim = keys_head.shape[1]

    def advance(running, turn_index):
        key_block = lax.dynamic_slice_in_dim(keys_head, turn_index * block_rows, block_rows, 0)
        unit_keys = to_unit(key_block).astype(jnp.bfloat16)
        cosine = jnp.dot(unit_keys, cents_head.T, preferred_element_type=jnp.float32)
        raised = jnp.exp(SHARPNESS * (cosine - 1.0))
        weights = (raised / lax.optimization_barrier(jnp.sum(raised, axis=1, keepdims=True))).astype(jnp.bfloat16)
        key_sums = running[0] + jnp.dot(weights.T, key_block, preferred_element_type=jnp.float32)
        if with_values:
            value_block = lax.dynamic_slice_in_dim(values_head, turn_index * block_rows, block_rows, 0)
            masses = running[1] + lax.optimization_barrier(jnp.sum(weights.astype(jnp.float32), axis=0))
            value_sums = running[2] + jnp.dot(weights.T, value_block, preferred_element_type=jnp.float32)
            return ((key_sums, masses, value_sums), None)
        return ((key_sums,), None)
    start = (jnp.zeros((cluster_count, head_dim), jnp.float32),)
    if with_values:
        start = (start[0], jnp.zeros((cluster_count,), jnp.float32), jnp.zeros((cluster_count, head_dim), jnp.float32))
    running, _ = lax.scan(advance, start, jnp.arange(turn_count, dtype=jnp.int32))
    return running

def decode_head(head, key_cache, value_cache, block_clusters, chosen_clusters, request_positions, queries, mean_keys, mean_values, log_mass):
    requests, group_size, head_dim = (queries.shape[0], queries.shape[2], queries.shape[3])
    token_count = key_cache.shape[1]
    cluster_count = mean_keys.shape[1]
    score_scale = head_dim ** (-0.5)
    flat_queries = queries[:, head].reshape(requests * group_size, head_dim)
    exact = jnp.dot(flat_queries, key_cache[head].T, preferred_element_type=jnp.float32).reshape(requests, group_size, token_count) * score_scale
    block_pick = jnp.any(chosen_clusters[:, head, :, None] == block_clusters[head][None, None, :], axis=1)
    token_pick = jnp.repeat(block_pick, BLOCK, axis=1) & (jnp.arange(token_count, dtype=jnp.int32)[None, :] < request_positions[:, None])
    summary = jnp.dot(flat_queries, mean_keys[head].T, preferred_element_type=jnp.float32).reshape(requests, group_size, cluster_count) * score_scale
    summary = summary + log_mass[head][None, None, :]
    summary_pick = jnp.logical_not(jnp.any(chosen_clusters[:, head, :, None] == jnp.arange(cluster_count, dtype=jnp.int32)[None, None, :], axis=1))
    exact_usable = token_pick[:, None, :]
    summary_usable = summary_pick[:, None, :]
    peak = jnp.maximum(lax.optimization_barrier(jnp.max(jnp.where(exact_usable, exact, NEGATIVE), axis=2)), lax.optimization_barrier(jnp.max(jnp.where(summary_usable, summary, NEGATIVE), axis=2)))
    exact_prob = jnp.where(exact_usable, jnp.exp(exact - peak[..., None]), 0.0).astype(jnp.bfloat16)
    summary_prob = jnp.where(summary_usable, jnp.exp(summary - peak[..., None]), 0.0).astype(jnp.bfloat16)
    weight_sum = lax.optimization_barrier(jnp.sum(exact_prob.astype(jnp.float32), axis=2)) + lax.optimization_barrier(jnp.sum(summary_prob.astype(jnp.float32), axis=2))
    weighted = jnp.dot(exact_prob.reshape(requests * group_size, token_count), value_cache[head], preferred_element_type=jnp.float32)
    weighted = weighted + jnp.dot(summary_prob.reshape(requests * group_size, cluster_count), mean_values[head], preferred_element_type=jnp.float32)
    weighted = weighted.reshape(requests, group_size, head_dim)
    return (weighted / weight_sum[..., None]).astype(jnp.bfloat16)

def reference(key_cache, value_cache, init_centroids, block_clusters, chosen_clusters, request_positions, queries):
    head_count = key_cache.shape[0]
    current = to_unit(init_centroids).astype(jnp.bfloat16)
    first_pass = jnp.stack([head_sums(key_cache[head], value_cache[head], current[head], False)[0] for head in range(head_count)])
    current = to_unit(first_pass).astype(jnp.bfloat16)
    second_pass = [head_sums(key_cache[head], value_cache[head], current[head], True) for head in range(head_count)]
    key_sums = jnp.stack([entry[0] for entry in second_pass])
    masses = jnp.stack([entry[1] for entry in second_pass])
    value_sums = jnp.stack([entry[2] for entry in second_pass])
    centroids = to_unit(key_sums)
    mean_keys = (key_sums / masses[..., None]).astype(jnp.bfloat16)
    mean_values = (value_sums / masses[..., None]).astype(jnp.bfloat16)
    log_mass = jnp.log(masses)
    attended = jnp.stack([decode_head(head, key_cache, value_cache, block_clusters, chosen_clusters, request_positions, queries, mean_keys, mean_values, log_mass) for head in range(head_count)], axis=1)
    return (centroids, attended)
```

```python
import functools
import math

import jax
import jax.numpy as jnp
from jax import lax
from jax.experimental import pallas as pl
from jax.experimental.pallas import tpu as pltpu
from jax.sharding import PartitionSpec as P

BLOCK = 128
SHARPNESS = 16.0
EPSILON = 1e-06
NEGATIVE = -1e30
MESH = pl.DeviceIdType.MESH
NT = (((1,), (1,)), ((), ()))
NN = (((1,), (0,)), ((), ()))


def to_unit(vectors):
    vectors = vectors.astype(jnp.float32)
    return (
        vectors
        * lax.rsqrt(jnp.mean(vectors * vectors, axis=-1, keepdims=True) + EPSILON)
        * vectors.shape[-1] ** (-0.5)
    )


def flipped(index, bits):
    bit = 1
    while bit <= bits:
        if bits & bit:
            index = index + bit * (1 - 2 * ((index // bit) % 2))
        bit *= 2
    return index


def dot(a, b, dims, precision=None):
    return lax.dot_general(a, b, dims, preferred_element_type=jnp.float32, precision=precision)


def kernel(
    n,
    tile,
    key_hbm, value_hbm, init_hbm, queries_hbm, chosen_hbm, blocks_hbm, positions_hbm,
    cent_out, att_out,
    queries_ref, chosen_ref, blocks_ref, positions_ref, init_v, keys, units, values, cents, held, sums, sums_k, sums_v, mass_acc, mass,
    first_a, first_half, first_b, keys_a, vals_a, mass_a, keys_half, vals_half, mass_half,
    keys_b, vals_b, mass_b, unit_cents, cent_in, parts, fin, att,
    local_sem, small_sem, k_send, k_recv, v_send, v_recv, a_send, a_recv, b_send, b_recv,
    g_send, g_recv, c_send, c_recv, f_send, f_recv, o_send, o_recv,
):
    heads, tok_dev, dim = key_hbm.shape
    requests, _, group, _ = queries_hbm.shape
    rows = requests * group
    members = n // heads
    chips = members // 2
    share = cents.shape[1]
    owned = share // heads
    tiles = tok_dev // tile
    clusters = members * share
    pieces, piece_rows = att.shape[1], att.shape[2]
    me = lax.axis_index("ctx")
    head, core, chip = (me // 2) % heads, me % 2, me // (2 * heads)
    member = chip * 2 + core
    other = 1 - core

    def at(of_head, of_member):
        return (of_member // 2) * (2 * heads) + of_head * 2 + of_member % 2


    barrier = pltpu.get_barrier_semaphore()
    partner = me + 1 - 2 * core
    peers = [partner]
    peers += [at(flipped(head, k), member) for k in range(1, heads)]
    peers += [at(head, (chip + d) % chips * 2 + core) for d in range(1, chips)]
    for peer in peers:
        pl.semaphore_signal(barrier, inc=1, device_id={"ctx": peer}, device_id_type=MESH)

    def remote(src, dst, send, recv, target):
        return pltpu.make_async_remote_copy(
            src_ref=src, dst_ref=dst, send_sem=send, recv_sem=recv,
            device_id={"ctx": target}, device_id_type=MESH,
        )

    init_copy = pltpu.make_async_copy(init_hbm.at[head], init_v, local_sem.at[0])
    key_copy = pltpu.make_async_copy(key_hbm.at[head], keys.at[0], local_sem.at[1])
    value_copy = pltpu.make_async_copy(value_hbm.at[head], values.at[0], local_sem.at[2])
    init_copy.start()
    key_copy.start()
    value_copy.start()
    small = (
        (queries_hbm, queries_ref), (chosen_hbm, chosen_ref),
        (blocks_hbm, blocks_ref), (positions_hbm, positions_ref),
    )
    small_copies = [
        pltpu.make_async_copy(source, here, small_sem.at[index])
        for index, (source, here) in enumerate(small)
    ]
    for copy in small_copies:
        copy.start()
    pl.semaphore_wait(barrier, len(peers))

    key_sends, value_sends = [], []
    for k in range(1, heads):
        to = flipped(head, k)
        key_sends.append(
            remote(key_hbm.at[to], keys.at[k], k_send.at[k], k_recv.at[k], at(to, member))
        )
        key_sends[-1].start()
    for k in range(1, heads):
        to = flipped(head, k)
        value_sends.append(
            remote(value_hbm.at[to], values.at[k], v_send.at[k], v_recv.at[k], at(to, member))
        )
        value_sends[-1].start()

    init_copy.wait()
    start = to_unit(init_v[...]).reshape(chips, heads, 2, owned, dim)
    for part in range(members):
        cents[part] = jnp.concatenate(
            [start[part // 2, s, part % 2] for s in range(heads)], axis=0
        ).astype(jnp.bfloat16)

    def weights_of(unit_keys, current):
        cosine = dot(current, unit_keys, NT)
        raised = jnp.exp2(cosine * (SHARPNESS * math.log2(math.e)))
        return raised * (1.0 / jnp.sum(raised, axis=0, keepdims=True))

    def scatter(stage, part, buffers, between=None):
        starts, halves, own = [], [], []
        for d in range(chips):
            place = (chip + d + 1) % chips
            for index, (term, (mine, came, _, _)) in enumerate(zip(part(place, other), buffers)):
                mine[place, other] = term
                starts.append(
                    remote(
                        mine.at[place, other], came.at[d], a_send.at[stage + index, d],
                        a_recv.at[stage + index, d], partner,
                    )
                )
                starts[-1].start()
            if between is not None and d == 0:
                between()
            for index, (term, (_, came, half, slots)) in enumerate(zip(part(place, core), buffers)):
                starts[d * len(buffers) + index].wait_recv()
                if d == chips - 1:
                    own.append(term + came[d])
                    continue
                half[d] = (term + came[d]).astype(half.dtype)
                halves.append(
                    remote(
                        half.at[d], slots.at[d], b_send.at[stage + index, d],
                        b_recv.at[stage + index, d], at(head, place * 2 + core),
                    )
                )
                halves[-1].start()
        return own, starts, halves

    def arrived(own, halves, slots, index, count):
        for d in range(chips - 1):
            halves[d * count + index].wait_recv()
            own = own + slots[d].astype(jnp.float32)
        return own

    key_copy.wait()
    for k in range(heads):
        if k:
            key_sends[k - 1].wait_recv()
        unit = to_unit(keys[k]).astype(jnp.bfloat16)
        for j in range(tiles):
            units[k * tiles + j] = unit[j * tile : (j + 1) * tile]
        current = cents[...].reshape(clusters, dim)
        total = None
        for j in range(tiles):
            w = weights_of(unit[j * tile : (j + 1) * tile], current).astype(jnp.bfloat16)
            if k == heads - 1:
                held[j] = w.reshape(members, share, tile)
                continue
            term = dot(w, keys[k, j * tile : (j + 1) * tile], NN)
            total = term if total is None else total + term
        if k < heads - 1:
            total = total.reshape(chips, 2, share, dim)
            sums[...] = total if k == 0 else sums[...] + total

    def first_part(place, side):
        total = sums[place, side]
        for j in range(tiles):
            total = total + dot(
                held[j, place * 2 + side], keys[heads - 1, j * tile : (j + 1) * tile], NN
            )
        return (total,)

    (own,), first_starts, first_halves = scatter(
        0, first_part, ((sums, first_a, first_half, first_b),)
    )

    own = arrived(own, first_halves, first_b, 0, 1)
    unit_cents[member] = to_unit(own).astype(jnp.bfloat16)
    gathers = []

    def share_out(place, index, target):
        piece = unit_cents.at[place]
        gathers.append(remote(piece, piece, g_send.at[index], g_recv.at[index], target))
        gathers[-1].start()

    for d in range(1, chips):
        share_out(member, d, at(head, (chip + d) % chips * 2 + core))
    share_out(member, chips, partner)

    for copy in small_copies:
        copy.wait()
    row_ids = lax.broadcasted_iota(jnp.int32, (rows, 1), 0)
    seen = jnp.zeros((rows, 1), jnp.int32)
    for r in range(requests):
        seen = jnp.where(row_ids // group == r, positions_ref[r], seen)
    chosen = chosen_ref[:, 0, :]
    for s in range(1, heads):
        chosen = jnp.where(head == s, chosen_ref[:, s, :], chosen)
    ksel = chosen.shape[1]
    chosen = jnp.broadcast_to(chosen[:, None, :], (requests, group, ksel)).reshape(rows, ksel)
    query = queries_ref[:, head].astype(jnp.float32).reshape(rows, dim).astype(jnp.bfloat16)
    scale = dim ** (-0.5)
    lanes = lax.broadcasted_iota(jnp.int32, (rows, BLOCK), 1)

    def exact_scores():
        found = []
        for k in range(heads):
            device = at(flipped(head, k), member)
            score = dot(query, keys[k], NT) * scale
            for b in range(tok_dev // BLOCK):
                cluster = blocks_ref[head, device * (tok_dev // BLOCK) + b]
                hits = jnp.max(jnp.where(chosen == cluster, 1, 0), axis=1, keepdims=True) > 0
                place = device * tok_dev + b * BLOCK + lanes
                usable = hits & (place < seen)
                found.append(
                    jnp.where(usable, score[:, b * BLOCK : (b + 1) * BLOCK], NEGATIVE)
                )
        return jnp.concatenate(found, axis=1)

    exact = exact_scores()
    exact_peak = jnp.max(exact, axis=1, keepdims=True)
    exact_prob = jnp.where(exact > 0.5 * NEGATIVE, jnp.exp(exact - exact_peak), 0.0).astype(
        jnp.bfloat16
    )
    exact_sum = jnp.sum(exact_prob.astype(jnp.float32), axis=1, keepdims=True)
    lane_ids = lax.broadcasted_iota(jnp.int32, (rows, share), 1)
    cluster_ids = at(lane_ids // owned, member) * owned + lane_ids % owned
    picked = chosen[:, 0:1] == cluster_ids
    for k in range(1, ksel):
        picked = picked | (chosen[:, k : k + 1] == cluster_ids)
    picked = jnp.where(picked, 1.0, 0.0)

    for d in range(1, chips):
        place = (chip + chips - d) % chips * 2 + core
        piece = unit_cents.at[place]
        remote(piece, piece, g_send.at[d], g_recv.at[d], partner).wait_recv()
        share_out(place, chips + d, partner)
    for d in range(chips):
        place = (chip + chips - d) % chips * 2 + other
        piece = unit_cents.at[place]
        remote(piece, piece, g_send.at[chips + d], g_recv.at[chips + d], partner).wait_recv()

    def second(k, light):
        current = unit_cents[...].reshape(clusters, dim)
        for j in range(tiles):
            w = weights_of(units[k * tiles + j], current)
            held[k * tiles + j] = w.astype(jnp.bfloat16).reshape(members, share, tile)
            for lane in range(0, tile, BLOCK):
                piece = w[:, lane : lane + BLOCK].reshape(members, share, BLOCK)
                mass_acc[...] += piece
        return light

    mass_acc[...] = jnp.zeros_like(mass_acc)
    lax.fori_loop(0, heads, second, 0)
    ones = jnp.ones((8, BLOCK), jnp.float32)
    for part in range(members):
        mass[part // 2, part % 2] = dot(ones, mass_acc[part], NT, lax.Precision.HIGHEST)
    value_copy.wait()
    for copy in value_sends:
        copy.wait_recv()

    def mass_part(place, side):
        return (mass[place, side],)

    def second_part(place, side):
        total = None
        for k in range(heads):
            for j in range(tiles):
                span = slice(j * tile, (j + 1) * tile)
                both = jnp.concatenate([keys[k, span], values[k, span]], axis=1)
                term = dot(held[k * tiles + j, place * 2 + side], both, NN)
                total = term if total is None else total + term
        return (total[:, :dim], total[:, dim:])

    mass_starts = []
    for d in range(1, chips + 1):
        place = (chip + d) % chips
        mass_starts.append(
            remote(
                mass.at[place, other], mass_a.at[d - 1], a_send.at[3, d - 1], a_recv.at[3, d - 1],
                partner,
            )
        )
        mass_starts[-1].start()
    mass_halves, mass_own = [], []

    def pass_masses():
        for d in range(1, chips + 1):
            place = (chip + d) % chips
            mass_starts[d - 1].wait_recv()
            total = mass[place, core] + mass_a[d - 1]
            if d == chips:
                mass_own.append(total)
                continue
            mass_half[d - 1] = total
            mass_halves.append(
                remote(
                    mass_half.at[d - 1], mass_b.at[d - 1], b_send.at[3, d - 1], b_recv.at[3, d - 1],
                    at(head, place * 2 + core),
                )
            )
            mass_halves[-1].start()

    (own_keys, own_values), second_starts, second_halves = scatter(
        1, second_part, ((sums_k, keys_a, keys_half, keys_b), (sums_v, vals_a, vals_half, vals_b)),
        pass_masses,
    )
    exact_weighted = dot(exact_prob, values[...].reshape(heads * tok_dev, dim), NN)
    own_keys = arrived(own_keys, second_halves, keys_b, 0, 2)
    cent_in[head] = to_unit(own_keys).reshape(heads, owned, dim)
    cent_sends = []
    for k in range(1, heads):
        to = flipped(head, k)
        cent_sends.append(
            remote(
                cent_in.at[head, to], cent_in.at[heads, k], c_send.at[k], c_recv.at[k],
                at(to, member),
            )
        )
        cent_sends[-1].start()
    own_mass = arrived(mass_own[0], mass_halves, mass_b, 0, 1)

    mass_row = own_mass[0:1]
    eye = lax.broadcasted_iota(jnp.int32, (share, share), 0) == lax.broadcasted_iota(
        jnp.int32, (share, share), 1
    )
    mass_column = jnp.sum(jnp.where(eye, mass_row, 0.0), axis=1, keepdims=True)
    mean_keys = (own_keys / mass_column).astype(jnp.bfloat16)
    score = dot(query, mean_keys, NT) * scale + jnp.log(mass_row)
    usable = picked < 0.5
    score = jnp.where(usable, score, NEGATIVE)
    peak = jnp.maximum(jnp.max(score, axis=1, keepdims=True), exact_peak)
    prob = jnp.where(usable, jnp.exp(score - peak), 0.0).astype(jnp.bfloat16)
    exact_factor = jnp.exp(exact_peak - peak)
    weight_sum = jnp.sum(prob.astype(jnp.float32), axis=1, keepdims=True) + exact_sum * exact_factor
    own_values = arrived(own_values, second_halves, vals_b, 1, 2)
    mean_values = (own_values / mass_column).astype(jnp.bfloat16)
    weighted = dot(prob, mean_values, NN) + exact_weighted * exact_factor
    shape = (pieces, piece_rows, dim)
    parts[:, 0] = weighted.reshape(shape)
    parts[:, 1] = jnp.broadcast_to(weight_sum, (rows, dim)).reshape(shape)
    parts[:, 2] = jnp.broadcast_to(peak, (rows, dim)).reshape(shape)

    def holds(index, action):
        if pieces == members:
            action()
        else:
            pl.when(index < pieces)(action)

    for d in range(1, members):
        to = (member + d) % members

        def give(to=to, d=d):
            remote(parts.at[to], fin.at[d], f_send.at[d], f_recv.at[d], at(head, to)).start()

        holds(to, give)

    def finish():
        for d in range(1, members):
            remote(parts.at[0], fin.at[d], f_send.at[d], f_recv.at[d], partner).wait_recv()
        stats = [parts[member]] + [fin[d] for d in range(1, members)]
        top = stats[0][2]
        for stat in stats[1:]:
            top = jnp.maximum(top, stat[2])
        upper, lower = 0.0, 0.0
        for stat in stats:
            factor = jnp.exp(stat[2] - top)
            upper = upper + stat[0] * factor
            lower = lower + stat[1] * factor
        att[head, member] = (upper / lower).astype(jnp.bfloat16)
        for d in range(1, n):
            to = (me + d) % n
            remote(
                att.at[head, member], att.at[head, member], o_send.at[d], o_recv.at[d], to
            ).start()

    holds(member, finish)

    for copy in cent_sends:
        copy.wait_recv()
    cent_out[head] = cent_in[head, head]
    for k in range(1, heads):
        source = flipped(head, k)
        cent_out[source] = cent_in[heads, k]

    for d in range(1, n):
        source = (me + n - d) % n

        def take(source=source, d=d):
            piece = att.at[(source // 2) % heads, source // (2 * heads) * 2 + source % 2]
            remote(piece, piece, o_send.at[d], o_recv.at[d], source).wait_recv()

        holds(source // (2 * heads) * 2 + source % 2, take)
    per = piece_rows // group
    for s in range(heads):
        for p in range(pieces):
            att_out[p * per : (p + 1) * per, s] = (
                att[s, p].astype(jnp.float32).reshape(per, group, dim).astype(jnp.bfloat16)
            )

    for copy in (
        key_sends + value_sends + first_starts + first_halves + gathers + mass_starts
        + mass_halves + second_starts + second_halves + cent_sends
    ):
        copy.wait_send()
    for d in range(1, members):
        to = (member + d) % members

        def gave(to=to, d=d):
            remote(parts.at[to], fin.at[d], f_send.at[d], f_recv.at[d], at(head, to)).wait_send()

        holds(to, gave)

    def told():
        piece = att.at[head, member]
        for d in range(1, n):
            remote(piece, piece, o_send.at[d], o_recv.at[d], (me + d) % n).wait_send()

    holds(member, told)


def put_out(cent_in, att_in, cent_out, att_out, sem):
    copies = (
        pltpu.make_async_copy(cent_in, cent_out, sem.at[0]),
        pltpu.make_async_copy(att_in, att_out, sem.at[1]),
    )
    for copy in copies:
        copy.start()
    for copy in copies:
        copy.wait()


def body(
    key_cache,
    value_cache,
    init_centroids,
    block_clusters,
    chosen_clusters,
    request_positions,
    queries,
):
    n = lax.axis_size("ctx")
    heads, tok_dev, dim = key_cache.shape
    requests, _, group, _ = queries.shape
    clusters = init_centroids.shape[1]
    members = n // heads
    chips = members // 2
    share = clusters // members
    owned = clusters // n
    piece_rows = max(group, requests * group // members)
    pieces = requests * group // piece_rows
    f32, bf16 = jnp.float32, jnp.bfloat16
    vmem, dma = pltpu.VMEM, pltpu.SemaphoreType.DMA
    anywhere = pl.BlockSpec(memory_space=pl.ANY)
    in_vmem = pl.BlockSpec(memory_space=pltpu.VMEM)
    half = (chips, share, dim)
    tile = math.gcd(256, tok_dev)
    tiles = tok_dev // tile
    results = (
        pl.pallas_call(
            functools.partial(kernel, n, tile),
            out_shape=(
                vmem((heads, owned, dim), f32),
                vmem(queries.shape, bf16),
            ),
            in_specs=[anywhere] * 7,
            out_specs=(in_vmem, in_vmem),
            scratch_shapes=[
                vmem(queries.shape, bf16),
                vmem(chosen_clusters.shape, jnp.int32),
                pltpu.SMEM(block_clusters.shape, jnp.int32),
                pltpu.SMEM(request_positions.shape, jnp.int32),
                vmem((clusters, dim), bf16),
                vmem((heads, tok_dev, dim), bf16),
                vmem((heads * tiles, tile, dim), bf16),
                vmem((heads, tok_dev, dim), bf16),
                vmem((members, share, dim), bf16),
                vmem((heads * tiles, members, share, tile), bf16),
                vmem((chips, 2, share, dim), f32),
                vmem((chips, 2, share, dim), f32),
                vmem((chips, 2, share, dim), f32),
                vmem((members, share, BLOCK), f32),
                vmem((chips, 2, 8, share), f32),
                vmem(half, f32),
                vmem(half, bf16),
                vmem(half, bf16),
                vmem(half, f32),
                vmem(half, f32),
                vmem((chips, 8, share), f32),
                vmem(half, bf16),
                vmem(half, bf16),
                vmem((chips, 8, share), f32),
                vmem(half, bf16),
                vmem(half, bf16),
                vmem((chips, 8, share), f32),
                vmem((members, share, dim), bf16),
                vmem((heads + 1, heads, owned, dim), f32),
                vmem((pieces, 3, piece_rows, dim), f32),
                vmem((members, 3, piece_rows, dim), f32),
                vmem((heads, pieces, piece_rows, dim), bf16),
                dma((3,)),
                dma((4,)),
                dma((heads,)),
                dma((heads,)),
                dma((heads,)),
                dma((heads,)),
                dma((4, chips)),
                dma((4, chips)),
                dma((4, chips)),
                dma((4, chips)),
                dma((members,)),
                dma((members,)),
                dma((heads,)),
                dma((heads,)),
                dma((members,)),
                dma((members,)),
                dma((n,)),
                dma((n,)),
            ],
            compiler_params=pltpu.CompilerParams(
                collective_id=0, has_side_effects=True, vmem_limit_bytes=56 * 1024 * 1024
            ),
        )(
            key_cache,
            value_cache,
            init_centroids,
            queries,
            chosen_clusters,
            block_clusters,
            request_positions,
        )
    )
    return tuple(
        pl.pallas_call(
            put_out,
            out_shape=tuple(jax.ShapeDtypeStruct(x.shape, x.dtype) for x in results),
            in_specs=[anywhere, anywhere],
            out_specs=(anywhere, anywhere),
            scratch_shapes=[dma((2,))],
        )(*(pltpu.with_memory_space_constraint(x, pltpu.VMEM) for x in results))
    )


def solution(mesh):
    placed = (
        P(None, ("groups", "ctx"), None),
        P(None, ("groups", "ctx"), None),
        P(),
        P(None, "groups"),
        P("groups", None, None),
        P("groups"),
        P("groups", None, None, None),
    )
    return jax.shard_map(
        body,
        mesh=mesh,
        in_specs=placed,
        out_specs=(P(None, ("groups", "ctx"), None), P("groups", None, None, None)),
        check_vma=False,
    )
```

```python
import functools
import math

import jax
import jax.numpy as jnp
from jax import lax
from jax.experimental import pallas as pl
from jax.experimental.pallas import tpu as pltpu
from jax.sharding import PartitionSpec as P

BLOCK = 128
SHARPNESS = 16.0
EPSILON = 1e-06
NEGATIVE = -1e30
MESH = pl.DeviceIdType.MESH
NT = (((1,), (1,)), ((), ()))
NN = (((1,), (0,)), ((), ()))


def to_unit(vectors):
    vectors = vectors.astype(jnp.float32)
    return (
        vectors
        * lax.rsqrt(jnp.mean(vectors * vectors, axis=-1, keepdims=True) + EPSILON)
        * vectors.shape[-1] ** (-0.5)
    )


def flipped(index, bits):
    bit = 1
    while bit <= bits:
        if bits & bit:
            index = index + bit * (1 - 2 * ((index // bit) % 2))
        bit *= 2
    return index


def dot(a, b, dims, precision=None):
    return lax.dot_general(a, b, dims, preferred_element_type=jnp.float32, precision=precision)


def kernel(
    n,
    tile,
    key_hbm, value_hbm, init_hbm, queries_hbm, chosen_hbm, blocks_hbm, positions_hbm,
    cent_out, att_out,
    queries_ref, chosen_ref, blocks_ref, positions_ref, init_v, keys, units, values, cents, held,
    scaled, den, invs, sums, sums_k, sums_v, mass,
    first_a, first_half, first_b, keys_a, vals_a, mass_a, keys_half, vals_half, mass_half,
    keys_b, vals_b, mass_b, unit_cents, cent_in, parts, fin, att,
    local_sem, small_sem, k_send, k_recv, v_send, v_recv, a_send, a_recv, b_send, b_recv,
    g_send, g_recv, c_send, c_recv, f_send, f_recv, o_send, o_recv,
):
    heads, tok_dev, dim = key_hbm.shape
    requests, _, group, _ = queries_hbm.shape
    rows = requests * group
    members = n // heads
    chips = members // 2
    cuts, crow = first_a.shape[1], first_a.shape[2]
    share = cuts * crow
    owned = share // heads
    tiles = tok_dev // tile
    pieces, piece_rows = att.shape[1], att.shape[2]
    me = lax.axis_index("ctx")
    head, core, chip = (me // 2) % heads, me % 2, me // (2 * heads)
    member = chip * 2 + core
    other = 1 - core

    def at(of_head, of_member):
        return (of_member // 2) * (2 * heads) + of_head * 2 + of_member % 2

    barrier = pltpu.get_barrier_semaphore()
    partner = me + 1 - 2 * core
    peers = [partner]
    peers += [at(flipped(head, k), member) for k in range(1, heads)]
    peers += [at(head, (chip + d) % chips * 2 + core) for d in range(1, chips)]
    for peer in peers:
        pl.semaphore_signal(barrier, inc=1, device_id={"ctx": peer}, device_id_type=MESH)

    sent = []

    def remote(src, dst, send, recv, target):
        return pltpu.make_async_remote_copy(
            src_ref=src, dst_ref=dst, send_sem=send, recv_sem=recv,
            device_id={"ctx": target}, device_id_type=MESH,
        )

    def begin(*args):
        copy = remote(*args)
        copy.start()
        sent.append(copy)
        return copy

    init_copy = pltpu.make_async_copy(init_hbm.at[head], init_v, local_sem.at[0])
    key_copy = pltpu.make_async_copy(key_hbm.at[head], keys.at[0], local_sem.at[1])
    value_copy = pltpu.make_async_copy(value_hbm.at[head], values.at[0], local_sem.at[2])
    init_copy.start()
    key_copy.start()
    value_copy.start()
    small = (
        (queries_hbm, queries_ref), (chosen_hbm, chosen_ref),
        (blocks_hbm, blocks_ref), (positions_hbm, positions_ref),
    )
    small_copies = [
        pltpu.make_async_copy(source, here, small_sem.at[index])
        for index, (source, here) in enumerate(small)
    ]
    for copy in small_copies:
        copy.start()
    pl.semaphore_wait(barrier, len(peers))

    key_sends, value_sends = {}, []
    for k in range(1, heads):
        to = flipped(head, k)
        for j in range(tiles):
            span = pl.ds(j * tile, tile)
            key_sends[k, j] = begin(
                key_hbm.at[to, span], keys.at[k, span], k_send.at[k, j], k_recv.at[k, j],
                at(to, member),
            )

    def send_values(k):
        to = flipped(head, k)
        value_sends.append(
            begin(value_hbm.at[to], values.at[k], v_send.at[k], v_recv.at[k], at(to, member))
        )

    if heads > 1:
        send_values(1)

    init_copy.wait()
    start = to_unit(init_v[...]).reshape(chips, heads, 2, owned, dim)
    for part in range(members):
        rows_of = jnp.concatenate(
            [start[part // 2, s, part % 2] for s in range(heads)], axis=0
        ).astype(jnp.bfloat16)
        for c in range(cuts):
            cents[part * cuts + c] = rows_of[c * crow : (c + 1) * crow]

    def raised_of(current, unit_keys):
        cosine = dot(current, unit_keys, NT)
        return jnp.exp2(cosine * (SHARPNESS * math.log2(math.e)))

    def folded(raised):
        return jnp.sum(raised.reshape(raised.shape[0] // 8, 8, raised.shape[1]), axis=0)

    def inverse(folds):
        return 1.0 / jnp.sum(folds, axis=0, keepdims=True)

    def column(row):
        return jnp.broadcast_to(row, (dim, row.shape[1])).T

    per = max(1, min(members * cuts, 128 // crow))

    def span_of(t):
        return slice(t * tile, (t + 1) * tile)

    def block_of(k):
        return slice(k * tok_dev, (k + 1) * tok_dev)

    key_copy.wait()
    for k in range(heads):
        for j in range(tiles):
            t = k * tiles + j
            if k:
                key_sends[k, j].wait_recv()
            own_keys = keys[k, span_of(j)].astype(jnp.float32)
            unit = to_unit(own_keys).astype(jnp.bfloat16)
            units[t] = unit
            folds = None
            for g in range(0, members * cuts, per):
                raised = raised_of(cents[g : g + per].reshape(per * crow, dim), unit)
                held[g : g + per, :, span_of(t)] = raised.astype(jnp.bfloat16).reshape(
                    per, crow, tile
                )
                folds = folded(raised) if folds is None else folds + folded(raised)
            scaled[span_of(t), :dim] = (own_keys * column(inverse(folds))).astype(jnp.bfloat16)
        if k < heads - 1:
            for index in range(members * cuts):
                term = dot(held[index, :, block_of(k)], scaled[block_of(k), :dim], NN)
                sums[index] = term if k == 0 else sums[index] + term

    def first_part(place, side, c):
        index = (place * 2 + side) * cuts + c
        last = block_of(heads - 1)
        return sums[index] + dot(held[index, :, last], scaled[last, :dim], NN)

    first_own = []
    for d in range(chips):
        place = (chip + d + 1) % chips
        arrivals = []
        for c in range(cuts):
            index = (place * 2 + other) * cuts + c
            sums[index] = first_part(place, other, c)
            arrivals.append(
                begin(
                    sums.at[index], first_a.at[d, c], a_send.at[0, d, c], a_recv.at[0, d, c],
                    partner,
                )
            )
        for c in range(cuts):
            term = first_part(place, core, c)
            arrivals[c].wait_recv()
            term = term + first_a[d, c]
            if d == chips - 1:
                first_own.append(term)
                continue
            first_half[d, c] = term.astype(first_half.dtype)
            begin(
                first_half.at[d, c], first_b.at[d, c], b_send.at[0, d, c], b_recv.at[0, d, c],
                at(head, place * 2 + core),
            )

    for k in range(2, min(3, heads)):
        send_values(k)

    for copy in small_copies:
        copy.wait()
    row_ids = lax.broadcasted_iota(jnp.int32, (rows, 1), 0)
    seen = jnp.zeros((rows, 1), jnp.int32)
    for r in range(requests):
        seen = jnp.where(row_ids // group == r, positions_ref[r], seen)
    chosen = chosen_ref[:, 0, :]
    for s in range(1, heads):
        chosen = jnp.where(head == s, chosen_ref[:, s, :], chosen)
    ksel = chosen.shape[1]
    chosen = jnp.broadcast_to(chosen[:, None, :], (requests, group, ksel)).reshape(rows, ksel)
    query = queries_ref[:, head].astype(jnp.float32).reshape(rows, dim).astype(jnp.bfloat16)
    scale = dim ** (-0.5)
    lanes = lax.broadcasted_iota(jnp.int32, (rows, BLOCK), 1)

    def exact_scores():
        found = []
        for k in range(heads):
            device = at(flipped(head, k), member)
            score = dot(query, keys[k], NT) * scale
            for b in range(tok_dev // BLOCK):
                cluster = blocks_ref[head, device * (tok_dev // BLOCK) + b]
                hits = jnp.max(jnp.where(chosen == cluster, 1, 0), axis=1, keepdims=True) > 0
                place = device * tok_dev + b * BLOCK + lanes
                usable = hits & (place < seen)
                found.append(
                    jnp.where(usable, score[:, b * BLOCK : (b + 1) * BLOCK], NEGATIVE)
                )
        return jnp.concatenate(found, axis=1)

    exact = exact_scores()
    exact_peak = jnp.max(exact, axis=1, keepdims=True)
    exact_prob = jnp.where(exact > 0.5 * NEGATIVE, jnp.exp(exact - exact_peak), 0.0).astype(
        jnp.bfloat16
    )
    exact_sum = jnp.sum(exact_prob.astype(jnp.float32), axis=1, keepdims=True)
    lane_ids = lax.broadcasted_iota(jnp.int32, (rows, share), 1)
    cluster_ids = at(lane_ids // owned, member) * owned + lane_ids % owned
    picked = chosen[:, 0:1] == cluster_ids
    for k in range(1, ksel):
        picked = picked | (chosen[:, k : k + 1] == cluster_ids)
    picked = jnp.where(picked, 1.0, 0.0)

    den[...] = jnp.zeros_like(den)

    def weigh(index):
        for t in range(heads * tiles):
            raised = raised_of(unit_cents[index], units[t])
            held[index, :, span_of(t)] = raised.astype(jnp.bfloat16)
            den[t] += folded(raised)

    def gathered(place, slot, c):
        index = place * cuts + c
        piece = unit_cents.at[index]
        remote(piece, piece, g_send.at[slot, c], g_recv.at[slot, c], partner).wait_recv()
        return index

    def share_out(index, slot, c, target):
        piece = unit_cents.at[index]
        begin(piece, piece, g_send.at[slot, c], g_recv.at[slot, c], target)

    for c in range(cuts):
        own = first_own[c]
        for d in range(chips - 1):
            slot = first_b.at[d, c]
            remote(
                slot, slot, b_send.at[0, d, c], b_recv.at[0, d, c], partner
            ).wait_recv()
            own = own + first_b[d, c].astype(jnp.float32)
        index = member * cuts + c
        unit_cents[index] = to_unit(own).astype(jnp.bfloat16)
        for d in range(1, chips):
            share_out(index, d, c, at(head, (chip + d) % chips * 2 + core))
        share_out(index, chips, c, partner)
        if c == cuts - 1:
            for k in range(3, heads):
                send_values(k)
        weigh(index)
        weigh(gathered(chip * 2 + other, chips, c))
    for d in range(1, chips):
        place = (chip + chips - d) % chips * 2
        for c in range(cuts):
            index = gathered(place + core, d, c)
            share_out(index, chips + d, c, partner)
            weigh(index)
    for d in range(1, chips):
        place = (chip + chips - d) % chips * 2
        for c in range(cuts):
            weigh(gathered(place + other, chips + d, c))

    value_copy.wait()
    for copy in value_sends:
        copy.wait_recv()
    term_ids = lax.broadcasted_iota(jnp.int32, (invs.shape[1], tile), 0)
    for t in range(heads * tiles):
        k, j = t // tiles, t % tiles
        inv = inverse(den[t])
        high = inv.astype(jnp.bfloat16).astype(jnp.float32)
        invs[t] = jnp.where(
            term_ids == 0, high, jnp.where(term_ids == 1, inv - high, 0.0)
        ).astype(jnp.bfloat16)
        wide = column(inv)
        for side, source in enumerate((keys, values)):
            scaled[span_of(t), side * dim : (side + 1) * dim] = (
                source[k, span_of(j)].astype(jnp.float32) * wide
            ).astype(jnp.bfloat16)

    def second_part(place, side, c):
        total = dot(held[(place * 2 + side) * cuts + c], scaled[...], NN)
        return total[:, :dim], total[:, dim:]

    def mass_part(place, side, c):
        index = (place * 2 + side) * cuts + c
        total = None
        for t in range(heads * tiles):
            term = dot(invs[t], held[index, :, span_of(t)], NT)
            total = term if total is None else total + term
        return jnp.broadcast_to(total[0:1] + total[1:2], (8, crow))

    flows = ((sums_k, keys_a, keys_half, keys_b), (sums_v, vals_a, vals_half, vals_b))
    own_sums = [[None] * cuts, [None] * cuts]
    own_masses = None
    for d in range(chips):
        place = (chip + d + 1) % chips
        far = at(head, place * 2 + core)
        arrivals = {}
        for c in range(cuts):
            index = (place * 2 + other) * cuts + c
            for flow, (term, (mine, came, _, _)) in enumerate(
                zip(second_part(place, other, c), flows)
            ):
                mine[index] = term
                arrivals[flow, c] = begin(
                    mine.at[index], came.at[d, c], a_send.at[1 + flow, d, c],
                    a_recv.at[1 + flow, d, c], partner,
                )
        for c in range(cuts):
            mass[place, c] = mass_part(place, other, c)
        mass_arrival = begin(
            mass.at[place], mass_a.at[d], a_send.at[3, d, 0], a_recv.at[3, d, 0], partner
        )
        for c in range(cuts):
            terms = second_part(place, core, c)
            if c == cuts - 1:
                masses = [mass_part(place, core, e) for e in range(cuts)]
                mass_arrival.wait_recv()
                masses = [masses[e] + mass_a[d, e] for e in range(cuts)]
                if d == chips - 1:
                    own_masses = masses
                else:
                    for e in range(cuts):
                        mass_half[d, e] = masses[e]
                    begin(
                        mass_half.at[d], mass_b.at[d], b_send.at[3, d, 0], b_recv.at[3, d, 0], far
                    )
            for flow, (term, (_, came, half, slots)) in enumerate(zip(terms, flows)):
                arrivals[flow, c].wait_recv()
                term = term + came[d, c]
                if d == chips - 1:
                    own_sums[flow][c] = term
                    continue
                half[d, c] = term.astype(half.dtype)
                begin(
                    half.at[d, c], slots.at[d, c], b_send.at[1 + flow, d, c],
                    b_recv.at[1 + flow, d, c], far,
                )

    exact_weighted = dot(exact_prob, values[...].reshape(heads * tok_dev, dim), NN)

    def landed(slots, row, d, c):
        slot = slots.at[d, c]
        remote(slot, slot, b_send.at[row, d, c], b_recv.at[row, d, c], partner).wait_recv()

    for d in range(chips - 1):
        slot = mass_b.at[d]
        remote(slot, slot, b_send.at[3, d, 0], b_recv.at[3, d, 0], partner).wait_recv()
        own_masses = [own_masses[c] + mass_b[d, c] for c in range(cuts)]
    mass_row = jnp.concatenate([m[0:1] for m in own_masses], axis=1)
    log_mass = jnp.log(mass_row)
    eye = lax.broadcasted_iota(jnp.int32, (share, share), 0) == lax.broadcasted_iota(
        jnp.int32, (share, share), 1
    )
    mass_column = jnp.sum(jnp.where(eye, mass_row, 0.0), axis=1, keepdims=True)

    for c in range(cuts):
        for d in range(chips - 1):
            landed(keys_b, 1, d, c)
            own_sums[0][c] = own_sums[0][c] + keys_b[d, c].astype(jnp.float32)
    own_keys = jnp.concatenate(own_sums[0], axis=0)
    cent_in[head] = to_unit(own_keys).reshape(heads, owned, dim)
    cent_sends = []
    for k in range(1, heads):
        to = flipped(head, k)
        cent_sends.append(
            begin(
                cent_in.at[head, to], cent_in.at[heads, k], c_send.at[k], c_recv.at[k],
                at(to, member),
            )
        )

    mean_keys = (own_keys / mass_column).astype(jnp.bfloat16)
    score = dot(query, mean_keys, NT) * scale + log_mass
    usable = picked < 0.5
    score = jnp.where(usable, score, NEGATIVE)
    peak = jnp.maximum(jnp.max(score, axis=1, keepdims=True), exact_peak)
    prob = jnp.where(usable, jnp.exp(score - peak), 0.0).astype(jnp.bfloat16)
    exact_factor = jnp.exp(exact_peak - peak)
    weight_sum = jnp.sum(prob.astype(jnp.float32), axis=1, keepdims=True) + exact_sum * exact_factor
    shape = (pieces, piece_rows, dim)
    stat_lanes = lax.broadcasted_iota(jnp.int32, (rows, dim), 1)
    parts[:, 1] = jnp.where(stat_lanes < dim // 2, weight_sum, peak).reshape(shape)
    for c in range(cuts):
        for d in range(chips - 1):
            landed(vals_b, 2, d, c)
            own_sums[1][c] = own_sums[1][c] + vals_b[d, c].astype(jnp.float32)
    own_values = jnp.concatenate(own_sums[1], axis=0)
    mean_values = (own_values / mass_column).astype(jnp.bfloat16)
    weighted = dot(prob, mean_values, NN) + exact_weighted * exact_factor
    parts[:, 0] = weighted.reshape(shape)

    def holds(index, action):
        if pieces == members:
            action()
        else:
            pl.when(index < pieces)(action)

    for d in range(1, members):
        to = (member + d) % members

        def give(to=to, d=d):
            remote(parts.at[to], fin.at[d], f_send.at[d], f_recv.at[d], at(head, to)).start()

        holds(to, give)

    def finish():
        for d in range(1, members):
            remote(parts.at[0], fin.at[d], f_send.at[d], f_recv.at[d], partner).wait_recv()
        stats = [parts[member]] + [fin[d] for d in range(1, members)]
        peaks = [stat[1][:, dim - 1 :] for stat in stats]
        top = functools.reduce(jnp.maximum, peaks)
        upper, lower = 0.0, 0.0
        for stat, high in zip(stats, peaks):
            factor = jnp.exp(high - top)
            upper = upper + stat[0] * factor
            lower = lower + stat[1][:, :1] * factor
        att[head, member] = (upper / lower).astype(jnp.bfloat16)
        for d in range(1, n):
            to = (me + d) % n
            remote(
                att.at[head, member], att.at[head, member], o_send.at[d], o_recv.at[d], to
            ).start()

    holds(member, finish)

    for copy in cent_sends:
        copy.wait_recv()
    cent_out[head] = cent_in[head, head]
    for k in range(1, heads):
        source = flipped(head, k)
        cent_out[source] = cent_in[heads, k]

    for copy in sent:
        copy.wait_send()
    for d in range(1, members):
        to = (member + d) % members

        def gave(to=to, d=d):
            remote(parts.at[to], fin.at[d], f_send.at[d], f_recv.at[d], at(head, to)).wait_send()

        holds(to, gave)

    for d in range(1, n):
        source = (me + n - d) % n

        def take(source=source, d=d):
            piece = att.at[(source // 2) % heads, source // (2 * heads) * 2 + source % 2]
            remote(piece, piece, o_send.at[d], o_recv.at[d], source).wait_recv()

        holds(source // (2 * heads) * 2 + source % 2, take)
    per_piece = piece_rows // group
    for s in range(heads):
        for p in range(pieces):
            att_out[p * per_piece : (p + 1) * per_piece, s] = (
                att[s, p].astype(jnp.float32).reshape(per_piece, group, dim).astype(jnp.bfloat16)
            )

    def told():
        piece = att.at[head, member]
        for d in range(1, n):
            remote(piece, piece, o_send.at[d], o_recv.at[d], (me + d) % n).wait_send()

    holds(member, told)


def put_out(cent_in, att_in, cent_out, att_out, sem):
    copies = (
        pltpu.make_async_copy(cent_in, cent_out, sem.at[0]),
        pltpu.make_async_copy(att_in, att_out, sem.at[1]),
    )
    for copy in copies:
        copy.start()
    for copy in copies:
        copy.wait()


def body(
    key_cache,
    value_cache,
    init_centroids,
    block_clusters,
    chosen_clusters,
    request_positions,
    queries,
):
    n = lax.axis_size("ctx")
    heads, tok_dev, dim = key_cache.shape
    requests, _, group, _ = queries.shape
    clusters = init_centroids.shape[1]
    members = n // heads
    chips = members // 2
    share = clusters // members
    owned = clusters // n
    cuts = 2 if share % 256 == 0 else 1
    crow = share // cuts
    piece_rows = max(group, requests * group // members)
    pieces = requests * group // piece_rows
    f32, bf16 = jnp.float32, jnp.bfloat16
    vmem, dma = pltpu.VMEM, pltpu.SemaphoreType.DMA
    anywhere = pl.BlockSpec(memory_space=pl.ANY)
    in_vmem = pl.BlockSpec(memory_space=pltpu.VMEM)
    whole = (members * cuts, crow, dim)
    half = (chips, cuts, crow, dim)
    small = (chips, cuts, 8, crow)
    tile = math.gcd(256, tok_dev)
    tiles = tok_dev // tile
    tokens = heads * tok_dev
    results = pl.pallas_call(
        functools.partial(kernel, n, tile),
        out_shape=(
            vmem((heads, owned, dim), f32),
            vmem(queries.shape, bf16),
        ),
        in_specs=[anywhere] * 7,
        out_specs=(in_vmem, in_vmem),
        scratch_shapes=[
            vmem(queries.shape, bf16),
            vmem(chosen_clusters.shape, jnp.int32),
            pltpu.SMEM(block_clusters.shape, jnp.int32),
            pltpu.SMEM(request_positions.shape, jnp.int32),
            vmem((clusters, dim), bf16),
            vmem((heads, tok_dev, dim), bf16),
            vmem((heads * tiles, tile, dim), bf16),
            vmem((heads, tok_dev, dim), bf16),
            vmem(whole, bf16),
            vmem((members * cuts, crow, tokens), bf16),
            vmem((tokens, 2 * dim), bf16),
            vmem((heads * tiles, 8, tile), f32),
            vmem((heads * tiles, 16, tile), bf16),
            vmem(whole, f32),
            vmem(whole, f32),
            vmem(whole, f32),
            vmem(small, f32),
            vmem(half, f32),
            vmem(half, bf16),
            vmem(half, bf16),
            vmem(half, f32),
            vmem(half, f32),
            vmem(small, f32),
            vmem(half, bf16),
            vmem(half, bf16),
            vmem(small, f32),
            vmem(half, bf16),
            vmem(half, bf16),
            vmem(small, f32),
            vmem(whole, bf16),
            vmem((heads + 1, heads, owned, dim), f32),
            vmem((pieces, 2, piece_rows, dim), f32),
            vmem((members, 2, piece_rows, dim), f32),
            vmem((heads, pieces, piece_rows, dim), bf16),
            dma((3,)),
            dma((4,)),
            dma((heads, tiles)),
            dma((heads, tiles)),
            dma((heads,)),
            dma((heads,)),
            dma((4, chips, cuts)),
            dma((4, chips, cuts)),
            dma((4, chips, cuts)),
            dma((4, chips, cuts)),
            dma((2 * chips, cuts)),
            dma((2 * chips, cuts)),
            dma((heads,)),
            dma((heads,)),
            dma((members,)),
            dma((members,)),
            dma((n,)),
            dma((n,)),
        ],
        compiler_params=pltpu.CompilerParams(
            collective_id=0, has_side_effects=True, vmem_limit_bytes=56 * 1024 * 1024
        ),
    )(
        key_cache,
        value_cache,
        init_centroids,
        queries,
        chosen_clusters,
        block_clusters,
        request_positions,
    )
    return tuple(
        pl.pallas_call(
            put_out,
            out_shape=tuple(jax.ShapeDtypeStruct(x.shape, x.dtype) for x in results),
            in_specs=[anywhere, anywhere],
            out_specs=(anywhere, anywhere),
            scratch_shapes=[dma((2,))],
        )(*(pltpu.with_memory_space_constraint(x, pltpu.VMEM) for x in results))
    )


def solution(mesh):
    placed = (
        P(None, ("groups", "ctx"), None),
        P(None, ("groups", "ctx"), None),
        P(),
        P(None, "groups"),
        P("groups", None, None),
        P("groups"),
        P("groups", None, None, None),
    )
    return jax.shard_map(
        body,
        mesh=mesh,
        in_specs=placed,
        out_specs=(P(None, ("groups", "ctx"), None), P("groups", None, None, None)),
        check_vma=False,
    )
```

```python
import functools
import math

import jax
import jax.numpy as jnp
from jax import lax
from jax.experimental import pallas as pl
from jax.experimental.pallas import tpu as pltpu
from jax.sharding import PartitionSpec as P

BLOCK = 128
SHARPNESS = 16.0
EPSILON = 1e-06
NEGATIVE = -1e30
MESH = pl.DeviceIdType.MESH
NT = (((1,), (1,)), ((), ()))
NN = (((1,), (0,)), ((), ()))


def to_unit(vectors):
    vectors = vectors.astype(jnp.float32)
    return (
        vectors
        * lax.rsqrt(jnp.mean(vectors * vectors, axis=-1, keepdims=True) + EPSILON)
        * vectors.shape[-1] ** (-0.5)
    )


def flipped(index, bits):
    bit = 1
    while bit <= bits:
        if bits & bit:
            index = index + bit * (1 - 2 * ((index // bit) % 2))
        bit *= 2
    return index


def dot(a, b, dims, precision=None):
    return lax.dot_general(a, b, dims, preferred_element_type=jnp.float32, precision=precision)


def kernel(
    n,
    tile,
    key_hbm, value_hbm, init_hbm, queries_hbm, chosen_hbm, blocks_hbm, positions_hbm,
    cent_out, att_out,
    queries_ref, chosen_ref, blocks_ref, positions_ref, init_v, keys, units, values, cents, held,
    scaled, den, invs, sums, sums_k, sums_v, mass,
    first_a, first_half, first_b, keys_a, vals_a, mass_a, keys_half, vals_half, mass_half,
    keys_b, vals_b, mass_b, unit_cents, cent_in, parts, fin, att,
    local_sem, small_sem, k_send, k_recv, v_send, v_recv, a_send, a_recv, b_send, b_recv,
    g_send, g_recv, c_send, c_recv, f_send, f_recv, o_send, o_recv,
):
    heads, tok_dev, dim = key_hbm.shape
    requests, _, group, _ = queries_hbm.shape
    rows = requests * group
    members = n // heads
    chips = members // 2
    cuts, crow = first_a.shape[1], first_a.shape[2]
    share = cuts * crow
    owned = share // heads
    tiles = tok_dev // tile
    pieces, piece_rows = att.shape[1], att.shape[2]
    me = lax.axis_index("ctx")
    head, core, chip = (me // 2) % heads, me % 2, me // (2 * heads)
    member = chip * 2 + core
    other = 1 - core

    def at(of_head, of_member):
        return (of_member // 2) * (2 * heads) + of_head * 2 + of_member % 2

    barrier = pltpu.get_barrier_semaphore()
    partner = me + 1 - 2 * core
    peers = [partner]
    peers += [at(flipped(head, k), member) for k in range(1, heads)]
    peers += [at(head, (chip + d) % chips * 2 + core) for d in range(1, chips)]
    for peer in peers:
        pl.semaphore_signal(barrier, inc=1, device_id={"ctx": peer}, device_id_type=MESH)

    sent = []

    def remote(src, dst, send, recv, target):
        return pltpu.make_async_remote_copy(
            src_ref=src, dst_ref=dst, send_sem=send, recv_sem=recv,
            device_id={"ctx": target}, device_id_type=MESH,
        )

    def begin(*args):
        copy = remote(*args)
        copy.start()
        sent.append(copy)
        return copy

    init_copy = pltpu.make_async_copy(init_hbm.at[head], init_v, local_sem.at[0])
    key_copy = pltpu.make_async_copy(key_hbm.at[head], keys.at[0], local_sem.at[1])
    value_copy = pltpu.make_async_copy(value_hbm.at[head], values.at[0], local_sem.at[2])
    init_copy.start()
    key_copy.start()
    value_copy.start()
    small = (
        (queries_hbm, queries_ref), (chosen_hbm, chosen_ref),
        (blocks_hbm, blocks_ref), (positions_hbm, positions_ref),
    )
    small_copies = [
        pltpu.make_async_copy(source, here, small_sem.at[index])
        for index, (source, here) in enumerate(small)
    ]
    for copy in small_copies:
        copy.start()
    pl.semaphore_wait(barrier, len(peers))

    key_sends, value_sends = {}, []
    for k in range(1, heads):
        to = flipped(head, k)
        for j in range(tiles):
            span = pl.ds(j * tile, tile)
            key_sends[k, j] = begin(
                key_hbm.at[to, span], keys.at[k, span], k_send.at[k, j], k_recv.at[k, j],
                at(to, member),
            )

    def send_values(k):
        to = flipped(head, k)
        value_sends.append(
            begin(value_hbm.at[to], values.at[k], v_send.at[k], v_recv.at[k], at(to, member))
        )

    init_copy.wait()
    start = to_unit(init_v[...]).reshape(chips, heads, 2, owned, dim)
    for part in range(members):
        rows_of = jnp.concatenate(
            [start[part // 2, s, part % 2] for s in range(heads)], axis=0
        ).astype(jnp.bfloat16)
        for c in range(cuts):
            cents[part * cuts + c] = rows_of[c * crow : (c + 1) * crow]

    def raised_of(current, unit_keys):
        cosine = dot(current, unit_keys, NT)
        return jnp.exp2(cosine * (SHARPNESS * math.log2(math.e)))

    def folded(raised):
        return jnp.sum(raised.reshape(raised.shape[0] // 8, 8, raised.shape[1]), axis=0)

    def inverse(folds):
        return 1.0 / jnp.sum(folds, axis=0, keepdims=True)

    def column(row):
        return jnp.broadcast_to(row, (dim, row.shape[1])).T

    per = max(1, min(members * cuts, 128 // crow))

    def span_of(t):
        return slice(t * tile, (t + 1) * tile)

    def block_of(k):
        return slice(k * tok_dev, (k + 1) * tok_dev)

    key_copy.wait()
    for k in range(heads):
        for j in range(tiles):
            t = k * tiles + j
            if k:
                key_sends[k, j].wait_recv()
            own_keys = keys[k, span_of(j)].astype(jnp.float32)
            unit = to_unit(own_keys).astype(jnp.bfloat16)
            units[t] = unit
            folds = None
            for g in range(0, members * cuts, per):
                raised = raised_of(cents[g : g + per].reshape(per * crow, dim), unit)
                held[g : g + per, :, span_of(t)] = raised.astype(jnp.bfloat16).reshape(
                    per, crow, tile
                )
                folds = folded(raised) if folds is None else folds + folded(raised)
            scaled[span_of(t), :dim] = (own_keys * column(inverse(folds))).astype(jnp.bfloat16)
        if k == 1 and heads > 2:
            send_values(2)
        if k < heads - 1:
            for index in range(members * cuts):
                term = dot(held[index, :, block_of(k)], scaled[block_of(k), :dim], NN)
                sums[index] = term if k == 0 else sums[index] + term

    if heads > 1:
        send_values(1)

    def first_part(place, side, c):
        index = (place * 2 + side) * cuts + c
        last = block_of(heads - 1)
        return sums[index] + dot(held[index, :, last], scaled[last, :dim], NN)

    first_own = []
    for d in range(chips):
        place = (chip + d + 1) % chips
        arrivals = []
        for c in range(cuts):
            index = (place * 2 + other) * cuts + c
            sums[index] = first_part(place, other, c)
            arrivals.append(
                begin(
                    sums.at[index], first_a.at[d, c], a_send.at[0, d, c], a_recv.at[0, d, c],
                    partner,
                )
            )
        for c in range(cuts):
            term = first_part(place, core, c)
            arrivals[c].wait_recv()
            term = term + first_a[d, c]
            if d == chips - 1:
                first_own.append(term)
                continue
            first_half[d, c] = term.astype(first_half.dtype)
            begin(
                first_half.at[d, c], first_b.at[d, c], b_send.at[0, d, c], b_recv.at[0, d, c],
                at(head, place * 2 + core),
            )

    for k in range(3, heads):
        send_values(k)

    for copy in small_copies:
        copy.wait()
    row_ids = lax.broadcasted_iota(jnp.int32, (rows, 1), 0)
    seen = jnp.zeros((rows, 1), jnp.int32)
    for r in range(requests):
        seen = jnp.where(row_ids // group == r, positions_ref[r], seen)
    chosen = chosen_ref[:, 0, :]
    for s in range(1, heads):
        chosen = jnp.where(head == s, chosen_ref[:, s, :], chosen)
    ksel = chosen.shape[1]
    chosen = jnp.broadcast_to(chosen[:, None, :], (requests, group, ksel)).reshape(rows, ksel)
    query = queries_ref[:, head].astype(jnp.float32).reshape(rows, dim).astype(jnp.bfloat16)
    scale = dim ** (-0.5)
    lanes = lax.broadcasted_iota(jnp.int32, (rows, BLOCK), 1)

    def exact_scores():
        found = []
        for k in range(heads):
            device = at(flipped(head, k), member)
            score = dot(query, keys[k], NT) * scale
            for b in range(tok_dev // BLOCK):
                cluster = blocks_ref[head, device * (tok_dev // BLOCK) + b]
                hits = jnp.max(jnp.where(chosen == cluster, 1, 0), axis=1, keepdims=True) > 0
                place = device * tok_dev + b * BLOCK + lanes
                usable = hits & (place < seen)
                found.append(
                    jnp.where(usable, score[:, b * BLOCK : (b + 1) * BLOCK], NEGATIVE)
                )
        return jnp.concatenate(found, axis=1)

    exact = exact_scores()
    exact_peak = jnp.max(exact, axis=1, keepdims=True)
    exact_prob = jnp.where(exact > 0.5 * NEGATIVE, jnp.exp(exact - exact_peak), 0.0).astype(
        jnp.bfloat16
    )
    exact_sum = jnp.sum(exact_prob.astype(jnp.float32), axis=1, keepdims=True)
    lane_ids = lax.broadcasted_iota(jnp.int32, (rows, share), 1)
    cluster_ids = at(lane_ids // owned, member) * owned + lane_ids % owned
    picked = chosen[:, 0:1] == cluster_ids
    for k in range(1, ksel):
        picked = picked | (chosen[:, k : k + 1] == cluster_ids)
    picked = jnp.where(picked, 1.0, 0.0)

    den[...] = jnp.zeros_like(den)

    def weigh(index):
        for t in range(heads * tiles):
            raised = raised_of(unit_cents[index], units[t])
            held[index, :, span_of(t)] = raised.astype(jnp.bfloat16)
            den[t] += folded(raised)

    def gathered(place, slot, c):
        index = place * cuts + c
        piece = unit_cents.at[index]
        remote(piece, piece, g_send.at[slot, c], g_recv.at[slot, c], partner).wait_recv()
        return index

    def share_out(index, slot, c, target):
        piece = unit_cents.at[index]
        begin(piece, piece, g_send.at[slot, c], g_recv.at[slot, c], target)

    for c in range(cuts):
        own = first_own[c]
        for d in range(chips - 1):
            slot = first_b.at[d, c]
            remote(
                slot, slot, b_send.at[0, d, c], b_recv.at[0, d, c], partner
            ).wait_recv()
            own = own + first_b[d, c].astype(jnp.float32)
        index = member * cuts + c
        unit_cents[index] = to_unit(own).astype(jnp.bfloat16)
        for d in range(1, chips):
            share_out(index, d, c, at(head, (chip + d) % chips * 2 + core))
        share_out(index, chips, c, partner)
        weigh(index)
        weigh(gathered(chip * 2 + other, chips, c))
    for d in range(1, chips):
        place = (chip + chips - d) % chips * 2
        for c in range(cuts):
            index = gathered(place + core, d, c)
            share_out(index, chips + d, c, partner)
            weigh(index)
    for d in range(1, chips):
        place = (chip + chips - d) % chips * 2
        for c in range(cuts):
            weigh(gathered(place + other, chips + d, c))

    value_copy.wait()
    for copy in value_sends:
        copy.wait_recv()
    term_ids = lax.broadcasted_iota(jnp.int32, (invs.shape[1], tile), 0)
    for t in range(heads * tiles):
        k, j = t // tiles, t % tiles
        inv = inverse(den[t])
        high = inv.astype(jnp.bfloat16).astype(jnp.float32)
        invs[t] = jnp.where(
            term_ids == 0, high, jnp.where(term_ids == 1, inv - high, 0.0)
        ).astype(jnp.bfloat16)
        wide = column(inv)
        for side, source in enumerate((keys, values)):
            scaled[span_of(t), side * dim : (side + 1) * dim] = (
                source[k, span_of(j)].astype(jnp.float32) * wide
            ).astype(jnp.bfloat16)

    def second_part(place, side, c):
        total = dot(held[(place * 2 + side) * cuts + c], scaled[...], NN)
        return total[:, :dim], total[:, dim:]

    def mass_part(place, side, c):
        index = (place * 2 + side) * cuts + c
        total = None
        for t in range(heads * tiles):
            term = dot(invs[t], held[index, :, span_of(t)], NT)
            total = term if total is None else total + term
        return jnp.broadcast_to(total[0:1] + total[1:2], (8, crow))

    flows = ((sums_k, keys_a, keys_half, keys_b), (sums_v, vals_a, vals_half, vals_b))
    own_sums = [[None] * cuts, [None] * cuts]
    own_masses = None
    for d in range(chips):
        place = (chip + d + 1) % chips
        far = at(head, place * 2 + core)
        arrivals = {}
        for c in range(cuts):
            index = (place * 2 + other) * cuts + c
            for flow, (term, (mine, came, _, _)) in enumerate(
                zip(second_part(place, other, c), flows)
            ):
                mine[index] = term
                arrivals[flow, c] = begin(
                    mine.at[index], came.at[d, c], a_send.at[1 + flow, d, c],
                    a_recv.at[1 + flow, d, c], partner,
                )
        for c in range(cuts):
            mass[place, c] = mass_part(place, other, c)
        mass_arrival = begin(
            mass.at[place], mass_a.at[d], a_send.at[3, d, 0], a_recv.at[3, d, 0], partner
        )
        for c in range(cuts):
            terms = second_part(place, core, c)
            if c == cuts - 1:
                masses = [mass_part(place, core, e) for e in range(cuts)]
                mass_arrival.wait_recv()
                masses = [masses[e] + mass_a[d, e] for e in range(cuts)]
                if d == chips - 1:
                    own_masses = masses
                else:
                    for e in range(cuts):
                        mass_half[d, e] = masses[e]
                    begin(
                        mass_half.at[d], mass_b.at[d], b_send.at[3, d, 0], b_recv.at[3, d, 0], far
                    )
            for flow, (term, (_, came, half, slots)) in enumerate(zip(terms, flows)):
                arrivals[flow, c].wait_recv()
                term = term + came[d, c]
                if d == chips - 1:
                    own_sums[flow][c] = term
                    continue
                half[d, c] = term.astype(half.dtype)
                begin(
                    half.at[d, c], slots.at[d, c], b_send.at[1 + flow, d, c],
                    b_recv.at[1 + flow, d, c], far,
                )

    exact_weighted = dot(exact_prob, values[...].reshape(heads * tok_dev, dim), NN)

    def landed(slots, row, d, c):
        slot = slots.at[d, c]
        remote(slot, slot, b_send.at[row, d, c], b_recv.at[row, d, c], partner).wait_recv()

    for d in range(chips - 1):
        slot = mass_b.at[d]
        remote(slot, slot, b_send.at[3, d, 0], b_recv.at[3, d, 0], partner).wait_recv()
        own_masses = [own_masses[c] + mass_b[d, c] for c in range(cuts)]
    mass_row = jnp.concatenate([m[0:1] for m in own_masses], axis=1)
    log_mass = jnp.log(mass_row)
    eye = lax.broadcasted_iota(jnp.int32, (share, share), 0) == lax.broadcasted_iota(
        jnp.int32, (share, share), 1
    )
    mass_column = jnp.sum(jnp.where(eye, mass_row, 0.0), axis=1, keepdims=True)

    for c in range(cuts):
        for d in range(chips - 1):
            landed(keys_b, 1, d, c)
            own_sums[0][c] = own_sums[0][c] + keys_b[d, c].astype(jnp.float32)
    own_keys = jnp.concatenate(own_sums[0], axis=0)
    cent_in[head] = to_unit(own_keys).reshape(heads, owned, dim)
    cent_sends = []
    for k in range(1, heads):
        to = flipped(head, k)
        cent_sends.append(
            begin(
                cent_in.at[head, to], cent_in.at[heads, k], c_send.at[k], c_recv.at[k],
                at(to, member),
            )
        )

    mean_keys = (own_keys / mass_column).astype(jnp.bfloat16)
    score = dot(query, mean_keys, NT) * scale + log_mass
    usable = picked < 0.5
    score = jnp.where(usable, score, NEGATIVE)
    peak = jnp.maximum(jnp.max(score, axis=1, keepdims=True), exact_peak)
    prob = jnp.where(usable, jnp.exp(score - peak), 0.0).astype(jnp.bfloat16)
    exact_factor = jnp.exp(exact_peak - peak)
    weight_sum = jnp.sum(prob.astype(jnp.float32), axis=1, keepdims=True) + exact_sum * exact_factor
    shape = (pieces, piece_rows, dim)
    stat_lanes = lax.broadcasted_iota(jnp.int32, (rows, dim), 1)
    parts[:, 1] = jnp.where(stat_lanes < dim // 2, weight_sum, peak).reshape(shape)
    for c in range(cuts):
        for d in range(chips - 1):
            landed(vals_b, 2, d, c)
            own_sums[1][c] = own_sums[1][c] + vals_b[d, c].astype(jnp.float32)
    own_values = jnp.concatenate(own_sums[1], axis=0)
    mean_values = (own_values / mass_column).astype(jnp.bfloat16)
    weighted = dot(prob, mean_values, NN) + exact_weighted * exact_factor
    parts[:, 0] = weighted.reshape(shape)

    def holds(index, action):
        if pieces == members:
            action()
        else:
            pl.when(index < pieces)(action)

    for d in range(1, members):
        to = (member + d) % members

        def give(to=to, d=d):
            remote(parts.at[to], fin.at[d], f_send.at[d], f_recv.at[d], at(head, to)).start()

        holds(to, give)

    def finish():
        for d in range(1, members):
            remote(parts.at[0], fin.at[d], f_send.at[d], f_recv.at[d], partner).wait_recv()
        stats = [parts[member]] + [fin[d] for d in range(1, members)]
        peaks = [stat[1][:, dim - 1 :] for stat in stats]
        top = functools.reduce(jnp.maximum, peaks)
        upper, lower = 0.0, 0.0
        for stat, high in zip(stats, peaks):
            factor = jnp.exp(high - top)
            upper = upper + stat[0] * factor
            lower = lower + stat[1][:, :1] * factor
        att[head, member] = (upper / lower).astype(jnp.bfloat16)
        for d in range(1, n):
            to = (me + d) % n
            remote(
                att.at[head, member], att.at[head, member], o_send.at[d], o_recv.at[d], to
            ).start()

    holds(member, finish)

    for copy in cent_sends:
        copy.wait_recv()
    cent_out[head] = cent_in[head, head]
    for k in range(1, heads):
        source = flipped(head, k)
        cent_out[source] = cent_in[heads, k]

    for copy in sent:
        copy.wait_send()
    for d in range(1, members):
        to = (member + d) % members

        def gave(to=to, d=d):
            remote(parts.at[to], fin.at[d], f_send.at[d], f_recv.at[d], at(head, to)).wait_send()

        holds(to, gave)

    for d in range(1, n):
        source = (me + n - d) % n

        def take(source=source, d=d):
            piece = att.at[(source // 2) % heads, source // (2 * heads) * 2 + source % 2]
            remote(piece, piece, o_send.at[d], o_recv.at[d], source).wait_recv()

        holds(source // (2 * heads) * 2 + source % 2, take)
    per_piece = piece_rows // group
    for s in range(heads):
        for p in range(pieces):
            att_out[p * per_piece : (p + 1) * per_piece, s] = (
                att[s, p].astype(jnp.float32).reshape(per_piece, group, dim).astype(jnp.bfloat16)
            )

    def told():
        piece = att.at[head, member]
        for d in range(1, n):
            remote(piece, piece, o_send.at[d], o_recv.at[d], (me + d) % n).wait_send()

    holds(member, told)


def put_out(cent_in, att_in, cent_out, att_out, sem):
    copies = (
        pltpu.make_async_copy(cent_in, cent_out, sem.at[0]),
        pltpu.make_async_copy(att_in, att_out, sem.at[1]),
    )
    for copy in copies:
        copy.start()
    for copy in copies:
        copy.wait()


def body(
    key_cache,
    value_cache,
    init_centroids,
    block_clusters,
    chosen_clusters,
    request_positions,
    queries,
):
    n = lax.axis_size("ctx")
    heads, tok_dev, dim = key_cache.shape
    requests, _, group, _ = queries.shape
    clusters = init_centroids.shape[1]
    members = n // heads
    chips = members // 2
    share = clusters // members
    owned = clusters // n
    cuts = 2 if share % 256 == 0 else 1
    crow = share // cuts
    piece_rows = max(group, requests * group // members)
    pieces = requests * group // piece_rows
    f32, bf16 = jnp.float32, jnp.bfloat16
    vmem, dma = pltpu.VMEM, pltpu.SemaphoreType.DMA
    anywhere = pl.BlockSpec(memory_space=pl.ANY)
    in_vmem = pl.BlockSpec(memory_space=pltpu.VMEM)
    whole = (members * cuts, crow, dim)
    half = (chips, cuts, crow, dim)
    small = (chips, cuts, 8, crow)
    tile = math.gcd(256, tok_dev)
    tiles = tok_dev // tile
    tokens = heads * tok_dev
    results = pl.pallas_call(
        functools.partial(kernel, n, tile),
        out_shape=(
            vmem((heads, owned, dim), f32),
            vmem(queries.shape, bf16),
        ),
        in_specs=[anywhere] * 7,
        out_specs=(in_vmem, in_vmem),
        scratch_shapes=[
            vmem(queries.shape, bf16),
            vmem(chosen_clusters.shape, jnp.int32),
            pltpu.SMEM(block_clusters.shape, jnp.int32),
            pltpu.SMEM(request_positions.shape, jnp.int32),
            vmem((clusters, dim), bf16),
            vmem((heads, tok_dev, dim), bf16),
            vmem((heads * tiles, tile, dim), bf16),
            vmem((heads, tok_dev, dim), bf16),
            vmem(whole, bf16),
            vmem((members * cuts, crow, tokens), bf16),
            vmem((tokens, 2 * dim), bf16),
            vmem((heads * tiles, 8, tile), f32),
            vmem((heads * tiles, 16, tile), bf16),
            vmem(whole, f32),
            vmem(whole, f32),
            vmem(whole, f32),
            vmem(small, f32),
            vmem(half, f32),
            vmem(half, bf16),
            vmem(half, bf16),
            vmem(half, f32),
            vmem(half, f32),
            vmem(small, f32),
            vmem(half, bf16),
            vmem(half, bf16),
            vmem(small, f32),
            vmem(half, bf16),
            vmem(half, bf16),
            vmem(small, f32),
            vmem(whole, bf16),
            vmem((heads + 1, heads, owned, dim), f32),
            vmem((pieces, 2, piece_rows, dim), f32),
            vmem((members, 2, piece_rows, dim), f32),
            vmem((heads, pieces, piece_rows, dim), bf16),
            dma((3,)),
            dma((4,)),
            dma((heads, tiles)),
            dma((heads, tiles)),
            dma((heads,)),
            dma((heads,)),
            dma((4, chips, cuts)),
            dma((4, chips, cuts)),
            dma((4, chips, cuts)),
            dma((4, chips, cuts)),
            dma((2 * chips, cuts)),
            dma((2 * chips, cuts)),
            dma((heads,)),
            dma((heads,)),
            dma((members,)),
            dma((members,)),
            dma((n,)),
            dma((n,)),
        ],
        compiler_params=pltpu.CompilerParams(
            collective_id=0, has_side_effects=True, vmem_limit_bytes=56 * 1024 * 1024
        ),
    )(
        key_cache,
        value_cache,
        init_centroids,
        queries,
        chosen_clusters,
        block_clusters,
        request_positions,
    )
    return tuple(
        pl.pallas_call(
            put_out,
            out_shape=tuple(jax.ShapeDtypeStruct(x.shape, x.dtype) for x in results),
            in_specs=[anywhere, anywhere],
            out_specs=(anywhere, anywhere),
            scratch_shapes=[dma((2,))],
        )(*(pltpu.with_memory_space_constraint(x, pltpu.VMEM) for x in results))
    )


def solution(mesh):
    placed = (
        P(None, ("groups", "ctx"), None),
        P(None, ("groups", "ctx"), None),
        P(),
        P(None, "groups"),
        P("groups", None, None),
        P("groups"),
        P("groups", None, None, None),
    )
    return jax.shard_map(
        body,
        mesh=mesh,
        in_specs=placed,
        out_specs=(P(None, ("groups", "ctx"), None), P("groups", None, None, None)),
        check_vma=False,
    )
```

```python
import functools
import math

import jax
import jax.numpy as jnp
from jax import lax
from jax.experimental import pallas as pl
from jax.experimental.pallas import tpu as pltpu
from jax.sharding import PartitionSpec as P

BLOCK = 128
SHARPNESS = 16.0
EPSILON = 1e-06
NEGATIVE = -1e30
MESH = pl.DeviceIdType.MESH
NT = (((1,), (1,)), ((), ()))
NN = (((1,), (0,)), ((), ()))


def to_unit(vectors):
    vectors = vectors.astype(jnp.float32)
    return (
        vectors
        * lax.rsqrt(jnp.mean(vectors * vectors, axis=-1, keepdims=True) + EPSILON)
        * vectors.shape[-1] ** (-0.5)
    )


def flipped(index, bits):
    bit = 1
    while bit <= bits:
        if bits & bit:
            index = index + bit * (1 - 2 * ((index // bit) % 2))
        bit *= 2
    return index


def dot(a, b, dims, precision=None):
    return lax.dot_general(a, b, dims, preferred_element_type=jnp.float32, precision=precision)


def kernel(
    n,
    tile,
    key_hbm, value_hbm, init_hbm, queries_hbm, chosen_hbm, blocks_hbm, positions_hbm,
    cent_out, att_out,
    queries_ref, chosen_ref, blocks_ref, positions_ref, init_v, keys, units, values, cents, held,
    scaled, den, invs, sums, sums_k, sums_v, mass,
    first_a, first_half, first_b, keys_a, vals_a, mass_a, keys_half, vals_half, mass_half,
    keys_b, vals_b, mass_b, unit_cents, cent_in, stats, parts, fin_stats, fin, att,
    local_sem, small_sem, k_send, k_recv, v_send, v_recv, a_send, a_recv, b_send, b_recv,
    g_send, g_recv, c_send, c_recv, s_send, s_recv, f_send, f_recv, o_send, o_recv,
):
    heads, tok_dev, dim = key_hbm.shape
    requests, _, group, _ = queries_hbm.shape
    rows = requests * group
    members = n // heads
    chips = members // 2
    cuts, crow = first_a.shape[1], first_a.shape[2]
    share = cuts * crow
    owned = share // heads
    tiles = tok_dev // tile
    half_rows = rows // 2
    me = lax.axis_index("ctx")
    head, core, chip = (me // 2) % heads, me % 2, me // (2 * heads)
    member = chip * 2 + core
    other = 1 - core

    def at(of_head, of_member):
        return (of_member // 2) * (2 * heads) + of_head * 2 + of_member % 2

    barrier = pltpu.get_barrier_semaphore()
    partner = me + 1 - 2 * core
    peers = [partner]
    peers += [at(flipped(head, k), member) for k in range(1, heads)]
    peers += [at(head, (chip + d) % chips * 2 + core) for d in range(1, chips)]
    for peer in peers:
        pl.semaphore_signal(barrier, inc=1, device_id={"ctx": peer}, device_id_type=MESH)

    sent = []

    def remote(src, dst, send, recv, target):
        return pltpu.make_async_remote_copy(
            src_ref=src, dst_ref=dst, send_sem=send, recv_sem=recv,
            device_id={"ctx": target}, device_id_type=MESH,
        )

    def begin(*args):
        copy = remote(*args)
        copy.start()
        sent.append(copy)
        return copy

    init_copy = pltpu.make_async_copy(init_hbm.at[head], init_v, local_sem.at[0])
    key_copy = pltpu.make_async_copy(key_hbm.at[head], keys.at[0], local_sem.at[1])
    value_copy = pltpu.make_async_copy(value_hbm.at[head], values.at[0], local_sem.at[2])
    init_copy.start()
    key_copy.start()
    value_copy.start()
    small = (
        (queries_hbm, queries_ref), (chosen_hbm, chosen_ref),
        (blocks_hbm, blocks_ref), (positions_hbm, positions_ref),
    )
    small_copies = [
        pltpu.make_async_copy(source, here, small_sem.at[index])
        for index, (source, here) in enumerate(small)
    ]
    for copy in small_copies:
        copy.start()
    pl.semaphore_wait(barrier, len(peers))

    key_sends, value_sends = {}, []
    for k in range(1, heads):
        to = flipped(head, k)
        for j in range(tiles):
            span = pl.ds(j * tile, tile)
            key_sends[k, j] = begin(
                key_hbm.at[to, span], keys.at[k, span], k_send.at[k, j], k_recv.at[k, j],
                at(to, member),
            )

    def send_values(k):
        to = flipped(head, k)
        value_sends.append(
            begin(value_hbm.at[to], values.at[k], v_send.at[k], v_recv.at[k], at(to, member))
        )

    init_copy.wait()
    start = to_unit(init_v[...]).reshape(chips, heads, 2, owned, dim)
    for part in range(members):
        rows_of = jnp.concatenate(
            [start[part // 2, s, part % 2] for s in range(heads)], axis=0
        ).astype(jnp.bfloat16)
        for c in range(cuts):
            cents[part * cuts + c] = rows_of[c * crow : (c + 1) * crow]

    def raised_of(current, unit_keys):
        cosine = dot(current, unit_keys, NT)
        return jnp.exp2(cosine * (SHARPNESS * math.log2(math.e)))

    def folded(raised):
        return jnp.sum(raised.reshape(raised.shape[0] // 8, 8, raised.shape[1]), axis=0)

    def inverse(folds):
        return 1.0 / jnp.sum(folds, axis=0, keepdims=True)

    def column(row):
        return jnp.broadcast_to(row, (dim, row.shape[1])).T

    per = max(1, min(members * cuts, 128 // crow))

    def span_of(t):
        return slice(t * tile, (t + 1) * tile)

    def block_of(k):
        return slice(k * tok_dev, (k + 1) * tok_dev)

    key_copy.wait()
    for k in range(heads):
        for j in range(tiles):
            t = k * tiles + j
            if k:
                key_sends[k, j].wait_recv()
            own_keys = keys[k, span_of(j)].astype(jnp.float32)
            unit = to_unit(own_keys).astype(jnp.bfloat16)
            units[t] = unit
            folds = None
            for g in range(0, members * cuts, per):
                raised = raised_of(cents[g : g + per].reshape(per * crow, dim), unit)
                held[g : g + per, :, span_of(t)] = raised.astype(jnp.bfloat16).reshape(
                    per, crow, tile
                )
                folds = folded(raised) if folds is None else folds + folded(raised)
            scaled[span_of(t), :dim] = (own_keys * column(inverse(folds))).astype(jnp.bfloat16)
        if k == 1 and heads > 2:
            send_values(2)
        if k < heads - 1:
            for index in range(members * cuts):
                term = dot(held[index, :, block_of(k)], scaled[block_of(k), :dim], NN)
                sums[index] = term if k == 0 else sums[index] + term

    if heads > 1:
        send_values(1)

    def first_part(place, side, c):
        index = (place * 2 + side) * cuts + c
        last = block_of(heads - 1)
        return sums[index] + dot(held[index, :, last], scaled[last, :dim], NN)

    first_own = []
    for d in range(chips):
        place = (chip + d + 1) % chips
        arrivals = []
        for c in range(cuts):
            index = (place * 2 + other) * cuts + c
            sums[index] = first_part(place, other, c)
            arrivals.append(
                begin(
                    sums.at[index], first_a.at[d, c], a_send.at[0, d, c], a_recv.at[0, d, c],
                    partner,
                )
            )
        for c in range(cuts):
            term = first_part(place, core, c)
            arrivals[c].wait_recv()
            term = term + first_a[d, c]
            if d == chips - 1:
                first_own.append(term)
                continue
            first_half[d, c] = term.astype(first_half.dtype)
            begin(
                first_half.at[d, c], first_b.at[d, c], b_send.at[0, d, c], b_recv.at[0, d, c],
                at(head, place * 2 + core),
            )

    for k in range(3, heads):
        send_values(k)

    for copy in small_copies:
        copy.wait()
    row_ids = lax.broadcasted_iota(jnp.int32, (rows, 1), 0)
    seen = jnp.zeros((rows, 1), jnp.int32)
    for r in range(requests):
        seen = jnp.where(row_ids // group == r, positions_ref[r], seen)
    chosen = chosen_ref[:, 0, :]
    for s in range(1, heads):
        chosen = jnp.where(head == s, chosen_ref[:, s, :], chosen)
    ksel = chosen.shape[1]
    chosen = jnp.broadcast_to(chosen[:, None, :], (requests, group, ksel)).reshape(rows, ksel)
    query = queries_ref[:, head].astype(jnp.float32).reshape(rows, dim).astype(jnp.bfloat16)
    scale = dim ** (-0.5)
    lanes = lax.broadcasted_iota(jnp.int32, (rows, BLOCK), 1)

    def exact_scores():
        found = []
        for k in range(heads):
            device = at(flipped(head, k), member)
            score = dot(query, keys[k], NT) * scale
            for b in range(tok_dev // BLOCK):
                cluster = blocks_ref[head, device * (tok_dev // BLOCK) + b]
                hits = jnp.max(jnp.where(chosen == cluster, 1, 0), axis=1, keepdims=True) > 0
                place = device * tok_dev + b * BLOCK + lanes
                usable = hits & (place < seen)
                found.append(
                    jnp.where(usable, score[:, b * BLOCK : (b + 1) * BLOCK], NEGATIVE)
                )
        return jnp.concatenate(found, axis=1)

    exact = exact_scores()
    exact_peak = jnp.max(exact, axis=1, keepdims=True)
    exact_prob = jnp.where(exact > 0.5 * NEGATIVE, jnp.exp(exact - exact_peak), 0.0).astype(
        jnp.bfloat16
    )
    exact_sum = jnp.sum(exact_prob.astype(jnp.float32), axis=1, keepdims=True)
    lane_ids = lax.broadcasted_iota(jnp.int32, (rows, share), 1)
    cluster_ids = at(lane_ids // owned, member) * owned + lane_ids % owned
    picked = chosen[:, 0:1] == cluster_ids
    for k in range(1, ksel):
        picked = picked | (chosen[:, k : k + 1] == cluster_ids)
    picked = jnp.where(picked, 1.0, 0.0)

    den[...] = jnp.zeros_like(den)

    def weigh(index):
        for t in range(heads * tiles):
            raised = raised_of(unit_cents[index], units[t])
            held[index, :, span_of(t)] = raised.astype(jnp.bfloat16)
            den[t] += folded(raised)

    def gathered(place, slot, c):
        index = place * cuts + c
        piece = unit_cents.at[index]
        remote(piece, piece, g_send.at[slot, c], g_recv.at[slot, c], partner).wait_recv()
        return index

    def share_out(index, slot, c, target):
        piece = unit_cents.at[index]
        begin(piece, piece, g_send.at[slot, c], g_recv.at[slot, c], target)

    for c in range(cuts):
        own = first_own[c]
        for d in range(chips - 1):
            slot = first_b.at[d, c]
            remote(
                slot, slot, b_send.at[0, d, c], b_recv.at[0, d, c], partner
            ).wait_recv()
            own = own + first_b[d, c].astype(jnp.float32)
        index = member * cuts + c
        unit_cents[index] = to_unit(own).astype(jnp.bfloat16)
        for d in range(1, chips):
            share_out(index, d, c, at(head, (chip + d) % chips * 2 + core))
        share_out(index, chips, c, partner)
        weigh(index)
        weigh(gathered(chip * 2 + other, chips, c))
    for d in range(1, chips):
        place = (chip + chips - d) % chips * 2
        for c in range(cuts):
            index = gathered(place + core, d, c)
            share_out(index, chips + d, c, partner)
            weigh(index)
    for d in range(1, chips):
        place = (chip + chips - d) % chips * 2
        for c in range(cuts):
            weigh(gathered(place + other, chips + d, c))

    value_copy.wait()
    for copy in value_sends:
        copy.wait_recv()
    term_ids = lax.broadcasted_iota(jnp.int32, (invs.shape[1], tile), 0)
    for t in range(heads * tiles):
        k, j = t // tiles, t % tiles
        inv = inverse(den[t])
        high = inv.astype(jnp.bfloat16).astype(jnp.float32)
        invs[t] = jnp.where(
            term_ids == 0, high, jnp.where(term_ids == 1, inv - high, 0.0)
        ).astype(jnp.bfloat16)
        wide = column(inv)
        for side, source in enumerate((keys, values)):
            scaled[span_of(t), side * dim : (side + 1) * dim] = (
                source[k, span_of(j)].astype(jnp.float32) * wide
            ).astype(jnp.bfloat16)

    def second_part(place, side, c):
        total = dot(held[(place * 2 + side) * cuts + c], scaled[...], NN)
        return total[:, :dim], total[:, dim:]

    def mass_part(place, side, c):
        index = (place * 2 + side) * cuts + c
        total = None
        for t in range(heads * tiles):
            term = dot(invs[t], held[index, :, span_of(t)], NT)
            total = term if total is None else total + term
        return jnp.broadcast_to(total[0:1] + total[1:2], (8, crow))

    flows = ((sums_k, keys_a, keys_half, keys_b), (sums_v, vals_a, vals_half, vals_b))
    own_sums = [[None] * cuts, [None] * cuts]
    own_masses = None
    for d in range(chips):
        place = (chip + d + 1) % chips
        far = at(head, place * 2 + core)
        arrivals = {}
        for c in range(cuts):
            index = (place * 2 + other) * cuts + c
            for flow, (term, (mine, came, _, _)) in enumerate(
                zip(second_part(place, other, c), flows)
            ):
                mine[index] = term
                arrivals[flow, c] = begin(
                    mine.at[index], came.at[d, c], a_send.at[1 + flow, d, c],
                    a_recv.at[1 + flow, d, c], partner,
                )
        for c in range(cuts):
            mass[place, c] = mass_part(place, other, c)
        mass_arrival = begin(
            mass.at[place], mass_a.at[d], a_send.at[3, d, 0], a_recv.at[3, d, 0], partner
        )
        for c in range(cuts):
            terms = second_part(place, core, c)
            if c == cuts - 1:
                masses = [mass_part(place, core, e) for e in range(cuts)]
                mass_arrival.wait_recv()
                masses = [masses[e] + mass_a[d, e] for e in range(cuts)]
                if d == chips - 1:
                    own_masses = masses
                else:
                    for e in range(cuts):
                        mass_half[d, e] = masses[e]
                    begin(
                        mass_half.at[d], mass_b.at[d], b_send.at[3, d, 0], b_recv.at[3, d, 0], far
                    )
            for flow, (term, (_, came, half, slots)) in enumerate(zip(terms, flows)):
                arrivals[flow, c].wait_recv()
                term = term + came[d, c]
                if d == chips - 1:
                    own_sums[flow][c] = term
                    continue
                half[d, c] = term.astype(half.dtype)
                begin(
                    half.at[d, c], slots.at[d, c], b_send.at[1 + flow, d, c],
                    b_recv.at[1 + flow, d, c], far,
                )

    exact_weighted = dot(exact_prob, values[...].reshape(heads * tok_dev, dim), NN)

    def landed(slots, row, d, c):
        slot = slots.at[d, c]
        remote(slot, slot, b_send.at[row, d, c], b_recv.at[row, d, c], partner).wait_recv()

    for d in range(chips - 1):
        slot = mass_b.at[d]
        remote(slot, slot, b_send.at[3, d, 0], b_recv.at[3, d, 0], partner).wait_recv()
        own_masses = [own_masses[c] + mass_b[d, c] for c in range(cuts)]
    mass_row = jnp.concatenate([m[0:1] for m in own_masses], axis=1)
    log_mass = jnp.log(mass_row)
    eye = lax.broadcasted_iota(jnp.int32, (share, share), 0) == lax.broadcasted_iota(
        jnp.int32, (share, share), 1
    )
    mass_column = jnp.sum(jnp.where(eye, mass_row, 0.0), axis=1, keepdims=True)

    for c in range(cuts):
        for d in range(chips - 1):
            landed(keys_b, 1, d, c)
            own_sums[0][c] = own_sums[0][c] + keys_b[d, c].astype(jnp.float32)
    own_keys = jnp.concatenate(own_sums[0], axis=0)
    cent_in[head] = to_unit(own_keys).reshape(heads, owned, dim)
    cent_sends = []
    for k in range(1, heads):
        to = flipped(head, k)
        cent_sends.append(
            begin(
                cent_in.at[head, to], cent_in.at[heads, k], c_send.at[k], c_recv.at[k],
                at(to, member),
            )
        )

    mean_keys = (own_keys / mass_column).astype(jnp.bfloat16)
    score = dot(query, mean_keys, NT) * scale + log_mass
    usable = picked < 0.5
    score = jnp.where(usable, score, NEGATIVE)
    peak = jnp.maximum(jnp.max(score, axis=1, keepdims=True), exact_peak)
    prob = jnp.where(usable, jnp.exp(score - peak), 0.0).astype(jnp.bfloat16)
    exact_factor = jnp.exp(exact_peak - peak)
    weight_sum = jnp.sum(prob.astype(jnp.float32), axis=1, keepdims=True) + exact_sum * exact_factor
    weight_sum = jnp.maximum(weight_sum, 1e-30)
    log_total = peak + jnp.log(weight_sum)
    row_lanes = lax.broadcasted_iota(jnp.int32, (half_rows, stats.shape[2]), 1)
    row_subs = lax.broadcasted_iota(jnp.int32, (half_rows, stats.shape[2]), 0)
    for side in range(2):
        here = log_total[side * half_rows : (side + 1) * half_rows]
        line = jnp.sum(jnp.where(row_lanes == row_subs, here, 0.0), axis=0, keepdims=True)
        stats[side] = jnp.broadcast_to(line, stats.shape[1:])
    for c in range(cuts):
        for d in range(chips - 1):
            landed(vals_b, 2, d, c)
            own_sums[1][c] = own_sums[1][c] + vals_b[d, c].astype(jnp.float32)
    own_values = jnp.concatenate(own_sums[1], axis=0)
    mean_values = (own_values / mass_column).astype(jnp.bfloat16)
    weighted = dot(prob, mean_values, NN) + exact_weighted * exact_factor
    parts[...] = (weighted / weight_sum).astype(parts.dtype).reshape(parts.shape)

    for d in range(1, members):
        to = (member + d) % members
        side = to % 2
        target = at(head, to)
        begin(stats.at[side], fin_stats.at[d], s_send.at[d], s_recv.at[d], target)
        begin(parts.at[side], fin.at[d], f_send.at[d], f_recv.at[d], target)

    totals, means = [stats[core]], [parts[core].astype(jnp.float32)]
    for d in range(1, members):
        slot = fin_stats.at[d]
        remote(slot, slot, s_send.at[d], s_recv.at[d], partner).wait_recv()
        totals.append(fin_stats[d])
    totals = [
        jnp.sum(jnp.where(row_lanes == row_subs, total[0:1], 0.0), axis=1, keepdims=True)
        for total in totals
    ]
    top = functools.reduce(jnp.maximum, totals)
    factors = [jnp.exp(total - top) for total in totals]
    scale_down = 1.0 / functools.reduce(jnp.add, factors)
    for d in range(1, members):
        slot = fin.at[d]
        remote(slot, slot, f_send.at[d], f_recv.at[d], partner).wait_recv()
        means.append(fin[d].astype(jnp.float32))
    upper = functools.reduce(jnp.add, [mean * factor for mean, factor in zip(means, factors)])
    att[head, core] = (upper * scale_down).astype(jnp.bfloat16)
    near = [(k, c) for k in range(heads) for c in range(2)][1:]
    piece = att.at[head, core]
    for index, (k, c) in enumerate(near):
        target = at(flipped(head, k), chip * 2 + (core + c) % 2)
        begin(piece, piece, o_send.at[index], o_recv.at[index], target)

    for copy in cent_sends:
        copy.wait_recv()
    cent_out[head] = cent_in[head, head]
    for k in range(1, heads):
        source = flipped(head, k)
        cent_out[source] = cent_in[heads, k]

    per_half = half_rows // group

    def place_out(of_head, side):
        att_out[pl.ds(side * per_half, per_half), of_head] = (
            att[of_head, side].astype(jnp.float32).reshape(per_half, group, dim).astype(jnp.bfloat16)
        )

    place_out(head, core)
    for index, (k, c) in enumerate(near):
        source, side = flipped(head, k), (core + c) % 2
        piece = att.at[source, side]
        remote(piece, piece, o_send.at[index], o_recv.at[index], partner).wait_recv()
        place_out(source, side)
    for copy in sent:
        copy.wait_send()


def put_out(cent_in, att_in, cent_out, att_out, sem):
    copies = (
        pltpu.make_async_copy(cent_in, cent_out, sem.at[0]),
        pltpu.make_async_copy(att_in, att_out, sem.at[1]),
    )
    for copy in copies:
        copy.start()
    for copy in copies:
        copy.wait()


def body(
    key_cache,
    value_cache,
    init_centroids,
    block_clusters,
    chosen_clusters,
    request_positions,
    queries,
):
    n = lax.axis_size("ctx")
    heads, tok_dev, dim = key_cache.shape
    requests, _, group, _ = queries.shape
    clusters = init_centroids.shape[1]
    members = n // heads
    chips = members // 2
    share = clusters // members
    owned = clusters // n
    cuts = 2 if share % 256 == 0 else 1
    crow = share // cuts
    half_rows = requests * group // 2
    f32, bf16 = jnp.float32, jnp.bfloat16
    vmem, dma = pltpu.VMEM, pltpu.SemaphoreType.DMA
    anywhere = pl.BlockSpec(memory_space=pl.ANY)
    in_vmem = pl.BlockSpec(memory_space=pltpu.VMEM)
    whole = (members * cuts, crow, dim)
    half = (chips, cuts, crow, dim)
    small = (chips, cuts, 8, crow)
    tile = math.gcd(256, tok_dev)
    tiles = tok_dev // tile
    tokens = heads * tok_dev
    results = pl.pallas_call(
        functools.partial(kernel, n, tile),
        out_shape=(
            vmem((heads, owned, dim), f32),
            vmem(queries.shape, bf16),
        ),
        in_specs=[anywhere] * 7,
        out_specs=(in_vmem, in_vmem),
        scratch_shapes=[
            vmem(queries.shape, bf16),
            vmem(chosen_clusters.shape, jnp.int32),
            pltpu.SMEM(block_clusters.shape, jnp.int32),
            pltpu.SMEM(request_positions.shape, jnp.int32),
            vmem((clusters, dim), bf16),
            vmem((heads, tok_dev, dim), bf16),
            vmem((heads * tiles, tile, dim), bf16),
            vmem((heads, tok_dev, dim), bf16),
            vmem(whole, bf16),
            vmem((members * cuts, crow, tokens), bf16),
            vmem((tokens, 2 * dim), bf16),
            vmem((heads * tiles, 8, tile), f32),
            vmem((heads * tiles, 16, tile), bf16),
            vmem(whole, f32),
            vmem(whole, f32),
            vmem(whole, f32),
            vmem(small, f32),
            vmem(half, f32),
            vmem(half, bf16),
            vmem(half, bf16),
            vmem(half, f32),
            vmem(half, f32),
            vmem(small, f32),
            vmem(half, bf16),
            vmem(half, bf16),
            vmem(small, f32),
            vmem(half, bf16),
            vmem(half, bf16),
            vmem(small, f32),
            vmem(whole, bf16),
            vmem((heads + 1, heads, owned, dim), f32),
            vmem((2, 8, 128), f32),
            vmem((2, half_rows, dim), bf16),
            vmem((members, 8, 128), f32),
            vmem((members, half_rows, dim), bf16),
            vmem((heads, 2, half_rows, dim), bf16),
            dma((3,)),
            dma((4,)),
            dma((heads, tiles)),
            dma((heads, tiles)),
            dma((heads,)),
            dma((heads,)),
            dma((4, chips, cuts)),
            dma((4, chips, cuts)),
            dma((4, chips, cuts)),
            dma((4, chips, cuts)),
            dma((2 * chips, cuts)),
            dma((2 * chips, cuts)),
            dma((heads,)),
            dma((heads,)),
            dma((members,)),
            dma((members,)),
            dma((members,)),
            dma((members,)),
            dma((2 * heads,)),
            dma((2 * heads,)),
        ],
        compiler_params=pltpu.CompilerParams(
            collective_id=0, has_side_effects=True, vmem_limit_bytes=56 * 1024 * 1024
        ),
    )(
        key_cache,
        value_cache,
        init_centroids,
        queries,
        chosen_clusters,
        block_clusters,
        request_positions,
    )
    return tuple(
        pl.pallas_call(
            put_out,
            out_shape=tuple(jax.ShapeDtypeStruct(x.shape, x.dtype) for x in results),
            in_specs=[anywhere, anywhere],
            out_specs=(anywhere, anywhere),
            scratch_shapes=[dma((2,))],
        )(*(pltpu.with_memory_space_constraint(x, pltpu.VMEM) for x in results))
    )


def solution(mesh):
    placed = (
        P(None, ("groups", "ctx"), None),
        P(None, ("groups", "ctx"), None),
        P(),
        P(None, "groups"),
        P("groups", None, None),
        P("groups"),
        P("groups", None, None, None),
    )
    return jax.shard_map(
        body,
        mesh=mesh,
        in_specs=placed,
        out_specs=(P(None, ("groups", "ctx"), None), P("groups", None, None, None)),
        check_vma=False,
    )
```

```python
import functools
import math

import jax
import jax.numpy as jnp
from jax import lax
from jax.experimental import pallas as pl
from jax.experimental.pallas import tpu as pltpu
from jax.sharding import PartitionSpec as P

BLOCK = 128
SHARPNESS = 16.0
EPSILON = 1e-06
NEGATIVE = -1e30
MESH = pl.DeviceIdType.MESH
NT = (((1,), (1,)), ((), ()))
NN = (((1,), (0,)), ((), ()))


def to_unit(vectors):
    vectors = vectors.astype(jnp.float32)
    return (
        vectors
        * lax.rsqrt(jnp.mean(vectors * vectors, axis=-1, keepdims=True) + EPSILON)
        * vectors.shape[-1] ** (-0.5)
    )


def flipped(index, bits):
    bit = 1
    while bit <= bits:
        if bits & bit:
            index = index + bit * (1 - 2 * ((index // bit) % 2))
        bit *= 2
    return index


def dot(a, b, dims, precision=None):
    return lax.dot_general(a, b, dims, preferred_element_type=jnp.float32, precision=precision)


def kernel(
    n,
    tile,
    key_hbm, value_hbm, init_hbm, queries_hbm, chosen_hbm, blocks_hbm, positions_hbm,
    cent_out, att_out,
    queries_ref, chosen_ref, blocks_ref, positions_ref, init_v, keys, units, values, cents, held,
    scaled, den, invs, sums, sums_k, sums_v, mass,
    first_a, first_half, first_b, keys_a, vals_a, mass_a, keys_half, vals_half, mass_half,
    keys_b, vals_b, mass_b, unit_cents, cent_in, stats, parts, fin_stats, fin, att,
    local_sem, small_sem, seen_sem, k_send, k_recv, v_send, v_recv, a_send, a_recv, b_send, b_recv,
    g_send, g_recv, c_send, c_recv, s_send, s_recv, f_send, f_recv, o_send, o_recv,
):
    heads, tok_dev, dim = key_hbm.shape
    requests, _, group, _ = queries_hbm.shape
    rows = requests * group
    members = n // heads
    chips = members // 2
    cuts, crow = first_a.shape[1], first_a.shape[2]
    share = cuts * crow
    owned = share // heads
    tiles = tok_dev // tile
    half_rows = rows // 2
    me = lax.axis_index("ctx")
    core, chip = me % 2, me // (2 * heads)

    def mirrored(place, of_chip):
        half = heads // 2
        return place + (of_chip % 2) * half * (1 - 2 * (place // half % 2))

    head = mirrored((me // 2) % heads, chip)
    member = chip * 2 + core
    other = 1 - core

    def at(of_head, of_member):
        of_chip = of_member // 2
        return of_chip * (2 * heads) + mirrored(of_head, of_chip) * 2 + of_member % 2

    barrier = pltpu.get_barrier_semaphore()
    partner = me + 1 - 2 * core
    near_entry = chips == 2 and heads == 4
    peers = [partner]
    if near_entry:
        row = me // heads
        inner = (row == 1) | (row == 2)
        peers += [at(flipped(head, k), member) for k in (1, 2)]
    else:
        peers += [at(flipped(head, k), member) for k in range(1, heads)]
        peers += [at(head, (chip + d) % chips * 2 + core) for d in range(1, chips)]

    def signal(sem, target):
        pl.semaphore_signal(sem, inc=1, device_id={"ctx": target}, device_id_type=MESH)

    for peer in peers:
        signal(barrier, peer)
    greeted = len(peers)
    if near_entry:
        across = at(head, (1 - chip) * 2 + core)
        pl.when(inner)(lambda: signal(barrier, across))
        greeted = greeted + jnp.where(inner, 1, 0)

    sent = []

    def remote(src, dst, send, recv, target):
        return pltpu.make_async_remote_copy(
            src_ref=src, dst_ref=dst, send_sem=send, recv_sem=recv,
            device_id={"ctx": target}, device_id_type=MESH,
        )

    def begin(*args):
        copy = remote(*args)
        copy.start()
        sent.append(copy)
        return copy

    init_copy = pltpu.make_async_copy(init_hbm.at[head], init_v, local_sem.at[0])
    key_copy = pltpu.make_async_copy(key_hbm.at[head], keys.at[0], local_sem.at[1])
    value_copy = pltpu.make_async_copy(value_hbm.at[head], values.at[0], local_sem.at[2])
    init_copy.start()
    key_copy.start()
    value_copy.start()
    small = (
        (queries_hbm, queries_ref), (chosen_hbm, chosen_ref),
        (blocks_hbm, blocks_ref), (positions_hbm, positions_ref),
    )
    small_copies = [
        pltpu.make_async_copy(source, here, small_sem.at[index])
        for index, (source, here) in enumerate(small)
    ]
    for copy in small_copies:
        copy.start()
    pl.semaphore_wait(barrier, greeted)

    key_sends, value_sends = {}, []

    def send_keys(k):
        to = flipped(head, k)
        for j in range(tiles):
            span = pl.ds(j * tile, tile)
            key_sends[k, j] = begin(
                key_hbm.at[to, span], keys.at[k, span], k_send.at[k, j], k_recv.at[k, j],
                at(to, member),
            )

    for k in range(1, 3 if near_entry else heads):
        send_keys(k)
    if near_entry:
        signal(seen_sem.at[0], at(flipped(head, 1), member))
        pl.when(inner)(lambda: signal(seen_sem.at[1], across))

    def send_last_keys():
        pl.semaphore_wait(seen_sem.at[0], 1)
        send_keys(3)

        def tell_outer():
            pl.semaphore_wait(seen_sem.at[1], 1)
            signal(seen_sem.at[1], at(flipped(head, 2), member))

        pl.when(inner)(tell_outer)

    def send_values(k):
        to = flipped(head, k)
        value_sends.append(
            begin(value_hbm.at[to], values.at[k], v_send.at[k], v_recv.at[k], at(to, member))
        )

    init_copy.wait()
    start = to_unit(init_v[...]).reshape(chips, heads, 2, owned, dim)
    for part in range(members):
        rows_of = jnp.concatenate(
            [start[part // 2, mirrored(s, part // 2), part % 2] for s in range(heads)], axis=0
        ).astype(jnp.bfloat16)
        for c in range(cuts):
            cents[part * cuts + c] = rows_of[c * crow : (c + 1) * crow]

    def raised_of(current, unit_keys):
        cosine = dot(current, unit_keys, NT)
        return jnp.exp2(cosine * (SHARPNESS * math.log2(math.e)))

    def folded(raised):
        return jnp.sum(raised.reshape(raised.shape[0] // 8, 8, raised.shape[1]), axis=0)

    def inverse(folds):
        return 1.0 / jnp.sum(folds, axis=0, keepdims=True)

    def column(row):
        return jnp.broadcast_to(row, (dim, row.shape[1])).T

    per = max(1, min(members * cuts, 128 // crow))

    def span_of(t):
        return slice(t * tile, (t + 1) * tile)

    def block_of(k):
        return slice(k * tok_dev, (k + 1) * tok_dev)

    key_copy.wait()
    for k in range(heads):
        for j in range(tiles):
            t = k * tiles + j
            if near_entry and k == 0 and j == tiles - 1:
                send_last_keys()
            if k:
                key_sends[k, j].wait_recv()
            own_keys = keys[k, span_of(j)].astype(jnp.float32)
            unit = to_unit(own_keys).astype(jnp.bfloat16)
            units[t] = unit
            folds = None
            for g in range(0, members * cuts, per):
                raised = raised_of(cents[g : g + per].reshape(per * crow, dim), unit)
                held[g : g + per, :, span_of(t)] = raised.astype(jnp.bfloat16).reshape(
                    per, crow, tile
                )
                folds = folded(raised) if folds is None else folds + folded(raised)
            scaled[span_of(t), :dim] = (own_keys * column(inverse(folds))).astype(jnp.bfloat16)
        if k == 1 and heads > 2:
            send_values(2)
        if k < heads - 1:
            for index in range(members * cuts):
                term = dot(held[index, :, block_of(k)], scaled[block_of(k), :dim], NN)
                sums[index] = term if k == 0 else sums[index] + term

    if heads > 1:
        send_values(1)

    def first_part(place, side, c):
        index = (place * 2 + side) * cuts + c
        last = block_of(heads - 1)
        return sums[index] + dot(held[index, :, last], scaled[last, :dim], NN)

    if near_entry:
        pl.when(jnp.logical_not(inner))(lambda: pl.semaphore_wait(seen_sem.at[1], 1))
    first_own = []
    for d in range(chips):
        place = (chip + d + 1) % chips
        arrivals = []
        for c in range(cuts):
            index = (place * 2 + other) * cuts + c
            sums[index] = first_part(place, other, c)
            arrivals.append(
                begin(
                    sums.at[index], first_a.at[d, c], a_send.at[0, d, c], a_recv.at[0, d, c],
                    partner,
                )
            )
        for c in range(cuts):
            term = first_part(place, core, c)
            arrivals[c].wait_recv()
            term = term + first_a[d, c]
            if d == chips - 1:
                first_own.append(term)
                continue
            first_half[d, c] = term.astype(first_half.dtype)
            begin(
                first_half.at[d, c], first_b.at[d, c], b_send.at[0, d, c], b_recv.at[0, d, c],
                at(head, place * 2 + core),
            )

    for k in range(3, heads):
        send_values(k)

    for copy in small_copies:
        copy.wait()
    row_ids = lax.broadcasted_iota(jnp.int32, (rows, 1), 0)
    seen = jnp.zeros((rows, 1), jnp.int32)
    for r in range(requests):
        seen = jnp.where(row_ids // group == r, positions_ref[r], seen)
    chosen = chosen_ref[:, 0, :]
    for s in range(1, heads):
        chosen = jnp.where(head == s, chosen_ref[:, s, :], chosen)
    ksel = chosen.shape[1]
    chosen = jnp.broadcast_to(chosen[:, None, :], (requests, group, ksel)).reshape(rows, ksel)
    query = queries_ref[:, head].astype(jnp.float32).reshape(rows, dim).astype(jnp.bfloat16)
    scale = dim ** (-0.5)
    lanes = lax.broadcasted_iota(jnp.int32, (rows, BLOCK), 1)

    def exact_scores():
        found = []
        for k in range(heads):
            device = at(flipped(head, k), member)
            score = dot(query, keys[k], NT) * scale
            for b in range(tok_dev // BLOCK):
                cluster = blocks_ref[head, device * (tok_dev // BLOCK) + b]
                hits = jnp.max(jnp.where(chosen == cluster, 1, 0), axis=1, keepdims=True) > 0
                place = device * tok_dev + b * BLOCK + lanes
                usable = hits & (place < seen)
                found.append(
                    jnp.where(usable, score[:, b * BLOCK : (b + 1) * BLOCK], NEGATIVE)
                )
        return jnp.concatenate(found, axis=1)

    exact = exact_scores()
    exact_peak = jnp.max(exact, axis=1, keepdims=True)
    exact_prob = jnp.where(exact > 0.5 * NEGATIVE, jnp.exp(exact - exact_peak), 0.0).astype(
        jnp.bfloat16
    )
    exact_sum = jnp.sum(exact_prob.astype(jnp.float32), axis=1, keepdims=True)
    lane_ids = lax.broadcasted_iota(jnp.int32, (rows, share), 1)
    cluster_ids = at(lane_ids // owned, member) * owned + lane_ids % owned
    picked = chosen[:, 0:1] == cluster_ids
    for k in range(1, ksel):
        picked = picked | (chosen[:, k : k + 1] == cluster_ids)
    picked = jnp.where(picked, 1.0, 0.0)

    den[...] = jnp.zeros_like(den)

    def weigh(index):
        for t in range(heads * tiles):
            raised = raised_of(unit_cents[index], units[t])
            held[index, :, span_of(t)] = raised.astype(jnp.bfloat16)
            den[t] += folded(raised)

    def gathered(place, slot, c):
        index = place * cuts + c
        piece = unit_cents.at[index]
        remote(piece, piece, g_send.at[slot, c], g_recv.at[slot, c], partner).wait_recv()
        return index

    def share_out(index, slot, c, target):
        piece = unit_cents.at[index]
        begin(piece, piece, g_send.at[slot, c], g_recv.at[slot, c], target)

    for c in range(cuts):
        own = first_own[c]
        for d in range(chips - 1):
            slot = first_b.at[d, c]
            remote(
                slot, slot, b_send.at[0, d, c], b_recv.at[0, d, c], partner
            ).wait_recv()
            own = own + first_b[d, c].astype(jnp.float32)
        index = member * cuts + c
        unit_cents[index] = to_unit(own).astype(jnp.bfloat16)
        for d in range(1, chips):
            share_out(index, d, c, at(head, (chip + d) % chips * 2 + core))
        share_out(index, chips, c, partner)
        weigh(index)
        weigh(gathered(chip * 2 + other, chips, c))
    for d in range(1, chips):
        place = (chip + chips - d) % chips * 2
        for c in range(cuts):
            index = gathered(place + core, d, c)
            share_out(index, chips + d, c, partner)
            weigh(index)
    for d in range(1, chips):
        place = (chip + chips - d) % chips * 2
        for c in range(cuts):
            weigh(gathered(place + other, chips + d, c))

    value_copy.wait()
    for copy in value_sends:
        copy.wait_recv()
    term_ids = lax.broadcasted_iota(jnp.int32, (invs.shape[1], tile), 0)
    for t in range(heads * tiles):
        k, j = t // tiles, t % tiles
        inv = inverse(den[t])
        high = inv.astype(jnp.bfloat16).astype(jnp.float32)
        invs[t] = jnp.where(
            term_ids == 0, high, jnp.where(term_ids == 1, inv - high, 0.0)
        ).astype(jnp.bfloat16)
        wide = column(inv)
        for side, source in enumerate((keys, values)):
            scaled[span_of(t), side * dim : (side + 1) * dim] = (
                source[k, span_of(j)].astype(jnp.float32) * wide
            ).astype(jnp.bfloat16)

    def second_part(place, side, c):
        total = dot(held[(place * 2 + side) * cuts + c], scaled[...], NN)
        return total[:, :dim], total[:, dim:]

    def mass_part(place, side, c):
        index = (place * 2 + side) * cuts + c
        total = None
        for t in range(heads * tiles):
            term = dot(invs[t], held[index, :, span_of(t)], NT)
            total = term if total is None else total + term
        return jnp.broadcast_to(total[0:1] + total[1:2], (8, crow))

    flows = ((sums_k, keys_a, keys_half, keys_b), (sums_v, vals_a, vals_half, vals_b))
    own_sums = [[None] * cuts, [None] * cuts]
    own_masses = None
    for d in range(chips):
        place = (chip + d + 1) % chips
        far = at(head, place * 2 + core)
        arrivals = {}
        for c in range(cuts):
            index = (place * 2 + other) * cuts + c
            for flow, (term, (mine, came, _, _)) in enumerate(
                zip(second_part(place, other, c), flows)
            ):
                mine[index] = term
                arrivals[flow, c] = begin(
                    mine.at[index], came.at[d, c], a_send.at[1 + flow, d, c],
                    a_recv.at[1 + flow, d, c], partner,
                )
        for c in range(cuts):
            mass[place, c] = mass_part(place, other, c)
        mass_arrival = begin(
            mass.at[place], mass_a.at[d], a_send.at[3, d, 0], a_recv.at[3, d, 0], partner
        )
        for c in range(cuts):
            terms = second_part(place, core, c)
            if c == cuts - 1:
                masses = [mass_part(place, core, e) for e in range(cuts)]
                mass_arrival.wait_recv()
                masses = [masses[e] + mass_a[d, e] for e in range(cuts)]
                if d == chips - 1:
                    own_masses = masses
                else:
                    for e in range(cuts):
                        mass_half[d, e] = masses[e]
                    begin(
                        mass_half.at[d], mass_b.at[d], b_send.at[3, d, 0], b_recv.at[3, d, 0], far
                    )
            for flow, (term, (_, came, half, slots)) in enumerate(zip(terms, flows)):
                arrivals[flow, c].wait_recv()
                term = term + came[d, c]
                if d == chips - 1:
                    own_sums[flow][c] = term
                    continue
                half[d, c] = term.astype(half.dtype)
                begin(
                    half.at[d, c], slots.at[d, c], b_send.at[1 + flow, d, c],
                    b_recv.at[1 + flow, d, c], far,
                )

    exact_weighted = dot(exact_prob, values[...].reshape(heads * tok_dev, dim), NN)

    def landed(slots, row, d, c):
        slot = slots.at[d, c]
        remote(slot, slot, b_send.at[row, d, c], b_recv.at[row, d, c], partner).wait_recv()

    for d in range(chips - 1):
        slot = mass_b.at[d]
        remote(slot, slot, b_send.at[3, d, 0], b_recv.at[3, d, 0], partner).wait_recv()
        own_masses = [own_masses[c] + mass_b[d, c] for c in range(cuts)]
    mass_row = jnp.concatenate([m[0:1] for m in own_masses], axis=1)
    log_mass = jnp.log(mass_row)
    eye = lax.broadcasted_iota(jnp.int32, (share, share), 0) == lax.broadcasted_iota(
        jnp.int32, (share, share), 1
    )
    mass_column = jnp.sum(jnp.where(eye, mass_row, 0.0), axis=1, keepdims=True)

    for c in range(cuts):
        for d in range(chips - 1):
            landed(keys_b, 1, d, c)
            own_sums[0][c] = own_sums[0][c] + keys_b[d, c].astype(jnp.float32)
    own_keys = jnp.concatenate(own_sums[0], axis=0)
    cent_in[head] = to_unit(own_keys).reshape(heads, owned, dim)
    cent_sends = []
    for k in range(1, heads):
        to = flipped(head, k)
        cent_sends.append(
            begin(
                cent_in.at[head, to], cent_in.at[heads, k], c_send.at[k], c_recv.at[k],
                at(to, member),
            )
        )

    mean_keys = (own_keys / mass_column).astype(jnp.bfloat16)
    score = dot(query, mean_keys, NT) * scale + log_mass
    usable = picked < 0.5
    score = jnp.where(usable, score, NEGATIVE)
    peak = jnp.maximum(jnp.max(score, axis=1, keepdims=True), exact_peak)
    prob = jnp.where(usable, jnp.exp(score - peak), 0.0).astype(jnp.bfloat16)
    exact_factor = jnp.exp(exact_peak - peak)
    weight_sum = jnp.sum(prob.astype(jnp.float32), axis=1, keepdims=True) + exact_sum * exact_factor
    weight_sum = jnp.maximum(weight_sum, 1e-30)
    log_total = peak + jnp.log(weight_sum)
    row_lanes = lax.broadcasted_iota(jnp.int32, (half_rows, stats.shape[2]), 1)
    row_subs = lax.broadcasted_iota(jnp.int32, (half_rows, stats.shape[2]), 0)
    for side in range(2):
        here = log_total[side * half_rows : (side + 1) * half_rows]
        line = jnp.sum(jnp.where(row_lanes == row_subs, here, 0.0), axis=0, keepdims=True)
        stats[side] = jnp.broadcast_to(line, stats.shape[1:])
    for c in range(cuts):
        for d in range(chips - 1):
            landed(vals_b, 2, d, c)
            own_sums[1][c] = own_sums[1][c] + vals_b[d, c].astype(jnp.float32)
    own_values = jnp.concatenate(own_sums[1], axis=0)
    mean_values = (own_values / mass_column).astype(jnp.bfloat16)
    weighted = dot(prob, mean_values, NN) + exact_weighted * exact_factor
    parts[...] = (weighted / weight_sum).astype(parts.dtype).reshape(parts.shape)

    for d in range(1, members):
        to = (member + d) % members
        side = to % 2
        target = at(head, to)
        begin(stats.at[side], fin_stats.at[d], s_send.at[d], s_recv.at[d], target)
        begin(parts.at[side], fin.at[d], f_send.at[d], f_recv.at[d], target)

    totals, means = [stats[core]], [parts[core].astype(jnp.float32)]
    for d in range(1, members):
        slot = fin_stats.at[d]
        remote(slot, slot, s_send.at[d], s_recv.at[d], partner).wait_recv()
        totals.append(fin_stats[d])
    totals = [
        jnp.sum(jnp.where(row_lanes == row_subs, total[0:1], 0.0), axis=1, keepdims=True)
        for total in totals
    ]
    top = functools.reduce(jnp.maximum, totals)
    factors = [jnp.exp(total - top) for total in totals]
    scale_down = 1.0 / functools.reduce(jnp.add, factors)
    for d in range(1, members):
        slot = fin.at[d]
        remote(slot, slot, f_send.at[d], f_recv.at[d], partner).wait_recv()
        means.append(fin[d].astype(jnp.float32))
    upper = functools.reduce(jnp.add, [mean * factor for mean, factor in zip(means, factors)])
    att[head, core] = (upper * scale_down).astype(jnp.bfloat16)
    near = [(k, c) for k in range(heads) for c in range(2)][1:]
    piece = att.at[head, core]
    for index, (k, c) in enumerate(near):
        target = at(flipped(head, k), chip * 2 + (core + c) % 2)
        begin(piece, piece, o_send.at[index], o_recv.at[index], target)

    for copy in cent_sends:
        copy.wait_recv()
    cent_out[head] = cent_in[head, head]
    for k in range(1, heads):
        source = flipped(head, k)
        cent_out[source] = cent_in[heads, k]

    per_half = half_rows // group

    def place_out(of_head, side):
        att_out[pl.ds(side * per_half, per_half), of_head] = (
            att[of_head, side].astype(jnp.float32).reshape(per_half, group, dim).astype(jnp.bfloat16)
        )

    place_out(head, core)
    for copy in sent[: -len(near)]:
        copy.wait_send()
    for index, (k, c) in enumerate(near):
        source, side = flipped(head, k), (core + c) % 2
        piece = att.at[source, side]
        remote(piece, piece, o_send.at[index], o_recv.at[index], partner).wait_recv()
        place_out(source, side)
    for copy in sent[-len(near) :]:
        copy.wait_send()


def put_out(cent_in, att_in, cent_out, att_out, sem):
    copies = (
        pltpu.make_async_copy(cent_in, cent_out, sem.at[0]),
        pltpu.make_async_copy(att_in, att_out, sem.at[1]),
    )
    for copy in copies:
        copy.start()
    for copy in copies:
        copy.wait()


def body(
    key_cache,
    value_cache,
    init_centroids,
    block_clusters,
    chosen_clusters,
    request_positions,
    queries,
):
    n = lax.axis_size("ctx")
    heads, tok_dev, dim = key_cache.shape
    requests, _, group, _ = queries.shape
    clusters = init_centroids.shape[1]
    members = n // heads
    chips = members // 2
    share = clusters // members
    owned = clusters // n
    cuts = 2 if share % 256 == 0 else 1
    crow = share // cuts
    half_rows = requests * group // 2
    f32, bf16 = jnp.float32, jnp.bfloat16
    vmem, dma = pltpu.VMEM, pltpu.SemaphoreType.DMA
    anywhere = pl.BlockSpec(memory_space=pl.ANY)
    in_vmem = pl.BlockSpec(memory_space=pltpu.VMEM)
    whole = (members * cuts, crow, dim)
    half = (chips, cuts, crow, dim)
    small = (chips, cuts, 8, crow)
    tile = math.gcd(256, tok_dev)
    tiles = tok_dev // tile
    tokens = heads * tok_dev
    results = pl.pallas_call(
        functools.partial(kernel, n, tile),
        out_shape=(
            vmem((heads, owned, dim), f32),
            vmem(queries.shape, bf16),
        ),
        in_specs=[anywhere] * 7,
        out_specs=(in_vmem, in_vmem),
        scratch_shapes=[
            vmem(queries.shape, bf16),
            vmem(chosen_clusters.shape, jnp.int32),
            pltpu.SMEM(block_clusters.shape, jnp.int32),
            pltpu.SMEM(request_positions.shape, jnp.int32),
            vmem((clusters, dim), bf16),
            vmem((heads, tok_dev, dim), bf16),
            vmem((heads * tiles, tile, dim), bf16),
            vmem((heads, tok_dev, dim), bf16),
            vmem(whole, bf16),
            vmem((members * cuts, crow, tokens), bf16),
            vmem((tokens, 2 * dim), bf16),
            vmem((heads * tiles, 8, tile), f32),
            vmem((heads * tiles, 16, tile), bf16),
            vmem(whole, f32),
            vmem(whole, f32),
            vmem(whole, f32),
            vmem(small, f32),
            vmem(half, f32),
            vmem(half, bf16),
            vmem(half, bf16),
            vmem(half, f32),
            vmem(half, f32),
            vmem(small, f32),
            vmem(half, bf16),
            vmem(half, bf16),
            vmem(small, f32),
            vmem(half, bf16),
            vmem(half, bf16),
            vmem(small, f32),
            vmem(whole, bf16),
            vmem((heads + 1, heads, owned, dim), f32),
            vmem((2, 8, 128), f32),
            vmem((2, half_rows, dim), bf16),
            vmem((members, 8, 128), f32),
            vmem((members, half_rows, dim), bf16),
            vmem((heads, 2, half_rows, dim), bf16),
            dma((3,)),
            dma((4,)),
            pltpu.SemaphoreType.REGULAR((2,)),
            dma((heads, tiles)),
            dma((heads, tiles)),
            dma((heads,)),
            dma((heads,)),
            dma((4, chips, cuts)),
            dma((4, chips, cuts)),
            dma((4, chips, cuts)),
            dma((4, chips, cuts)),
            dma((2 * chips, cuts)),
            dma((2 * chips, cuts)),
            dma((heads,)),
            dma((heads,)),
            dma((members,)),
            dma((members,)),
            dma((members,)),
            dma((members,)),
            dma((2 * heads,)),
            dma((2 * heads,)),
        ],
        compiler_params=pltpu.CompilerParams(
            collective_id=0, has_side_effects=True, vmem_limit_bytes=56 * 1024 * 1024
        ),
    )(
        key_cache,
        value_cache,
        init_centroids,
        queries,
        chosen_clusters,
        block_clusters,
        request_positions,
    )
    return tuple(
        pl.pallas_call(
            put_out,
            out_shape=tuple(jax.ShapeDtypeStruct(x.shape, x.dtype) for x in results),
            in_specs=[anywhere, anywhere],
            out_specs=(anywhere, anywhere),
            scratch_shapes=[dma((2,))],
        )(*(pltpu.with_memory_space_constraint(x, pltpu.VMEM) for x in results))
    )


def solution(mesh):
    placed = (
        P(None, ("groups", "ctx"), None),
        P(None, ("groups", "ctx"), None),
        P(),
        P(None, "groups"),
        P("groups", None, None),
        P("groups"),
        P("groups", None, None, None),
    )
    return jax.shard_map(
        body,
        mesh=mesh,
        in_specs=placed,
        out_specs=(P(None, ("groups", "ctx"), None), P("groups", None, None, None)),
        check_vma=False,
    )
```

```python
import functools
import math

import jax
import jax.numpy as jnp
from jax import lax
from jax.experimental import pallas as pl
from jax.experimental.pallas import tpu as pltpu
from jax.sharding import PartitionSpec as P

BLOCK = 128
SHARPNESS = 16.0
EPSILON = 1e-06
NEGATIVE = -1e30
MESH = pl.DeviceIdType.MESH
NT = (((1,), (1,)), ((), ()))
NN = (((1,), (0,)), ((), ()))


def to_unit(vectors):
    vectors = vectors.astype(jnp.float32)
    return (
        vectors
        * lax.rsqrt(jnp.mean(vectors * vectors, axis=-1, keepdims=True) + EPSILON)
        * vectors.shape[-1] ** (-0.5)
    )


def flipped(index, bits):
    bit = 1
    while bit <= bits:
        if bits & bit:
            index = index + bit * (1 - 2 * ((index // bit) % 2))
        bit *= 2
    return index


def dot(a, b, dims, precision=None):
    return lax.dot_general(a, b, dims, preferred_element_type=jnp.float32, precision=precision)


def kernel(
    n,
    tile,
    key_hbm, value_hbm, init_hbm, queries_hbm, chosen_hbm, blocks_hbm, positions_hbm,
    cent_out, att_out,
    queries_ref, chosen_ref, blocks_ref, positions_ref, init_v, keys, units, values, cents, held,
    scaled, den, invs, sums, sums_k, sums_v, mass,
    first_a, first_half, first_b, keys_a, vals_a, mass_a, keys_half, vals_half, mass_half,
    keys_b, vals_b, mass_b, unit_cents, cent_in, stats, parts, fin_stats, fin, att,
    local_sem, small_sem, seen_sem, k_send, k_recv, v_send, v_recv, a_send, a_recv, b_send, b_recv,
    g_send, g_recv, c_send, c_recv, s_send, s_recv, f_send, f_recv, o_send, o_recv,
):
    heads, tok_dev, dim = key_hbm.shape
    requests, _, group, _ = queries_hbm.shape
    rows = requests * group
    members = n // heads
    chips = members // 2
    cuts, crow = first_a.shape[1], first_a.shape[2]
    share = cuts * crow
    owned = share // heads
    tiles = tok_dev // tile
    half_rows = rows // 2
    me = lax.axis_index("ctx")
    core, chip = me % 2, me // (2 * heads)

    def mirrored(place, of_chip):
        half = heads // 2
        return place + (of_chip % 2) * half * (1 - 2 * (place // half % 2))

    head = mirrored((me // 2) % heads, chip)
    member = chip * 2 + core
    other = 1 - core

    def at(of_head, of_member):
        of_chip = of_member // 2
        return of_chip * (2 * heads) + mirrored(of_head, of_chip) * 2 + of_member % 2

    barrier = pltpu.get_barrier_semaphore()
    partner = me + 1 - 2 * core
    near_entry = chips == 2 and heads == 4
    peers = [partner]
    if near_entry:
        row = me // heads
        inner = (row == 1) | (row == 2)
        peers += [at(flipped(head, k), member) for k in (1, 2)]
    else:
        peers += [at(flipped(head, k), member) for k in range(1, heads)]
        peers += [at(head, (chip + d) % chips * 2 + core) for d in range(1, chips)]

    def signal(sem, target):
        pl.semaphore_signal(sem, inc=1, device_id={"ctx": target}, device_id_type=MESH)

    for peer in peers:
        signal(barrier, peer)
    greeted = len(peers)
    if near_entry:
        across = at(head, (1 - chip) * 2 + core)
        pl.when(inner)(lambda: signal(barrier, across))
        greeted = greeted + jnp.where(inner, 1, 0)

    sent = []

    def remote(src, dst, send, recv, target):
        return pltpu.make_async_remote_copy(
            src_ref=src, dst_ref=dst, send_sem=send, recv_sem=recv,
            device_id={"ctx": target}, device_id_type=MESH,
        )

    def begin(*args):
        copy = remote(*args)
        copy.start()
        sent.append(copy)
        return copy

    init_copy = pltpu.make_async_copy(init_hbm.at[head], init_v, local_sem.at[0])
    key_copy = pltpu.make_async_copy(key_hbm.at[head], keys.at[0], local_sem.at[1])
    value_copy = pltpu.make_async_copy(value_hbm.at[head], values.at[0], local_sem.at[2])
    init_copy.start()
    key_copy.start()
    value_copy.start()
    small = (
        (queries_hbm, queries_ref), (chosen_hbm, chosen_ref),
        (blocks_hbm, blocks_ref), (positions_hbm, positions_ref),
    )
    small_copies = [
        pltpu.make_async_copy(source, here, small_sem.at[index])
        for index, (source, here) in enumerate(small)
    ]
    for copy in small_copies:
        copy.start()
    pl.semaphore_wait(barrier, greeted)

    key_sends, value_sends = {}, []

    def send_keys(k):
        to = flipped(head, k)
        for j in range(tiles):
            span = pl.ds(j * tile, tile)
            key_sends[k, j] = begin(
                key_hbm.at[to, span], keys.at[k, span], k_send.at[k, j], k_recv.at[k, j],
                at(to, member),
            )

    for k in range(1, 3 if near_entry else heads):
        send_keys(k)
    if near_entry:
        signal(seen_sem.at[0], at(flipped(head, 1), member))
        pl.when(inner)(lambda: signal(seen_sem.at[1], across))

    def send_last_keys():
        pl.semaphore_wait(seen_sem.at[0], 1)
        send_keys(3)

        def tell_outer():
            pl.semaphore_wait(seen_sem.at[1], 1)
            signal(seen_sem.at[1], at(flipped(head, 2), member))

        pl.when(inner)(tell_outer)

    def send_values(k):
        to = flipped(head, k)
        value_sends.append(
            begin(value_hbm.at[to], values.at[k], v_send.at[k], v_recv.at[k], at(to, member))
        )

    init_copy.wait()
    start = to_unit(init_v[...]).reshape(chips, heads, 2, owned, dim)
    for part in range(members):
        rows_of = jnp.concatenate(
            [start[part // 2, mirrored(s, part // 2), part % 2] for s in range(heads)], axis=0
        ).astype(jnp.bfloat16)
        for c in range(cuts):
            cents[part * cuts + c] = rows_of[c * crow : (c + 1) * crow]

    def raised_of(current, unit_keys):
        cosine = dot(current, unit_keys, NT)
        return jnp.exp2(cosine * (SHARPNESS * math.log2(math.e)))

    def folded(raised):
        return jnp.sum(raised.reshape(raised.shape[0] // 8, 8, raised.shape[1]), axis=0)

    def inverse(folds):
        return 1.0 / jnp.sum(folds, axis=0, keepdims=True)

    def column(row):
        return jnp.broadcast_to(row, (dim, row.shape[1])).T

    per = max(1, min(members * cuts, 128 // crow))

    def span_of(t):
        return slice(t * tile, (t + 1) * tile)

    def block_of(k):
        return slice(k * tok_dev, (k + 1) * tok_dev)

    key_copy.wait()
    for k in range(heads):
        for j in range(tiles):
            t = k * tiles + j
            if near_entry and k == 0 and j == tiles - 1:
                send_last_keys()
            if k:
                key_sends[k, j].wait_recv()
            own_keys = keys[k, span_of(j)].astype(jnp.float32)
            unit = to_unit(own_keys).astype(jnp.bfloat16)
            units[t] = unit
            folds = None
            for g in range(0, members * cuts, per):
                raised = raised_of(cents[g : g + per].reshape(per * crow, dim), unit)
                held[g : g + per, :, span_of(t)] = raised.astype(jnp.bfloat16).reshape(
                    per, crow, tile
                )
                folds = folded(raised) if folds is None else folds + folded(raised)
            scaled[span_of(t), :dim] = (own_keys * column(inverse(folds))).astype(jnp.bfloat16)
        if k == 2 and heads > 2:
            send_values(2)
        if k < heads - 1:
            for index in range(members * cuts):
                term = dot(held[index, :, block_of(k)], scaled[block_of(k), :dim], NN)
                sums[index] = term if k == 0 else sums[index] + term

    if heads > 1:
        send_values(1)

    def first_part(place, side, c):
        index = (place * 2 + side) * cuts + c
        last = block_of(heads - 1)
        return sums[index] + dot(held[index, :, last], scaled[last, :dim], NN)

    if near_entry:
        pl.when(jnp.logical_not(inner))(lambda: pl.semaphore_wait(seen_sem.at[1], 1))
    first_own = []
    for d in range(chips):
        place = (chip + d + 1) % chips
        arrivals = []
        for c in range(cuts):
            index = (place * 2 + other) * cuts + c
            sums[index] = first_part(place, other, c)
            arrivals.append(
                begin(
                    sums.at[index], first_a.at[d, c], a_send.at[0, d, c], a_recv.at[0, d, c],
                    partner,
                )
            )
        for c in range(cuts):
            term = first_part(place, core, c)
            arrivals[c].wait_recv()
            term = term + first_a[d, c]
            if d == chips - 1:
                first_own.append(term)
                continue
            first_half[d, c] = term.astype(first_half.dtype)
            begin(
                first_half.at[d, c], first_b.at[d, c], b_send.at[0, d, c], b_recv.at[0, d, c],
                at(head, place * 2 + core),
            )

    for k in range(3, heads):
        send_values(k)

    for copy in small_copies:
        copy.wait()
    row_ids = lax.broadcasted_iota(jnp.int32, (rows, 1), 0)
    seen = jnp.zeros((rows, 1), jnp.int32)
    for r in range(requests):
        seen = jnp.where(row_ids // group == r, positions_ref[r], seen)
    chosen = chosen_ref[:, 0, :]
    for s in range(1, heads):
        chosen = jnp.where(head == s, chosen_ref[:, s, :], chosen)
    ksel = chosen.shape[1]
    chosen = jnp.broadcast_to(chosen[:, None, :], (requests, group, ksel)).reshape(rows, ksel)
    query = queries_ref[:, head].astype(jnp.float32).reshape(rows, dim).astype(jnp.bfloat16)
    scale = dim ** (-0.5)
    lanes = lax.broadcasted_iota(jnp.int32, (rows, BLOCK), 1)

    def exact_scores():
        found = []
        for k in range(heads):
            device = at(flipped(head, k), member)
            score = dot(query, keys[k], NT) * scale
            for b in range(tok_dev // BLOCK):
                cluster = blocks_ref[head, device * (tok_dev // BLOCK) + b]
                hits = jnp.max(jnp.where(chosen == cluster, 1, 0), axis=1, keepdims=True) > 0
                place = device * tok_dev + b * BLOCK + lanes
                usable = hits & (place < seen)
                found.append(
                    jnp.where(usable, score[:, b * BLOCK : (b + 1) * BLOCK], NEGATIVE)
                )
        return jnp.concatenate(found, axis=1)

    exact = exact_scores()
    exact_peak = jnp.max(exact, axis=1, keepdims=True)
    exact_prob = jnp.where(exact > 0.5 * NEGATIVE, jnp.exp(exact - exact_peak), 0.0).astype(
        jnp.bfloat16
    )
    exact_sum = jnp.sum(exact_prob.astype(jnp.float32), axis=1, keepdims=True)
    lane_ids = lax.broadcasted_iota(jnp.int32, (rows, share), 1)
    cluster_ids = at(lane_ids // owned, member) * owned + lane_ids % owned
    picked = chosen[:, 0:1] == cluster_ids
    for k in range(1, ksel):
        picked = picked | (chosen[:, k : k + 1] == cluster_ids)
    picked = jnp.where(picked, 1.0, 0.0)

    den[...] = jnp.zeros_like(den)

    def weigh(index):
        for t in range(heads * tiles):
            raised = raised_of(unit_cents[index], units[t])
            held[index, :, span_of(t)] = raised.astype(jnp.bfloat16)
            den[t] += folded(raised)

    def gathered(place, slot, c):
        index = place * cuts + c
        piece = unit_cents.at[index]
        remote(piece, piece, g_send.at[slot, c], g_recv.at[slot, c], partner).wait_recv()
        return index

    def share_out(index, slot, c, target):
        piece = unit_cents.at[index]
        begin(piece, piece, g_send.at[slot, c], g_recv.at[slot, c], target)

    for c in range(cuts):
        own = first_own[c]
        for d in range(chips - 1):
            slot = first_b.at[d, c]
            remote(
                slot, slot, b_send.at[0, d, c], b_recv.at[0, d, c], partner
            ).wait_recv()
            own = own + first_b[d, c].astype(jnp.float32)
        index = member * cuts + c
        unit_cents[index] = to_unit(own).astype(jnp.bfloat16)
        for d in range(1, chips):
            share_out(index, d, c, at(head, (chip + d) % chips * 2 + core))
        share_out(index, chips, c, partner)
        weigh(index)
        weigh(gathered(chip * 2 + other, chips, c))
    for d in range(1, chips):
        place = (chip + chips - d) % chips * 2
        for c in range(cuts):
            index = gathered(place + core, d, c)
            share_out(index, chips + d, c, partner)
            weigh(index)
    for d in range(1, chips):
        place = (chip + chips - d) % chips * 2
        for c in range(cuts):
            weigh(gathered(place + other, chips + d, c))

    value_copy.wait()
    for copy in value_sends:
        copy.wait_recv()
    term_ids = lax.broadcasted_iota(jnp.int32, (invs.shape[1], tile), 0)
    for t in range(heads * tiles):
        k, j = t // tiles, t % tiles
        inv = inverse(den[t])
        high = inv.astype(jnp.bfloat16).astype(jnp.float32)
        invs[t] = jnp.where(
            term_ids == 0, high, jnp.where(term_ids == 1, inv - high, 0.0)
        ).astype(jnp.bfloat16)
        wide = column(inv)
        for side, source in enumerate((keys, values)):
            scaled[span_of(t), side * dim : (side + 1) * dim] = (
                source[k, span_of(j)].astype(jnp.float32) * wide
            ).astype(jnp.bfloat16)

    def second_part(place, side, c):
        index, middle = (place * 2 + side) * cuts + c, heads * tok_dev // 2
        total = dot(held[index, :, :middle], scaled[:middle], NN) + dot(
            held[index, :, middle:], scaled[middle:], NN
        )
        return total[:, :dim], total[:, dim:]

    def mass_part(place, side, c):
        index = (place * 2 + side) * cuts + c
        total = None
        for t in range(heads * tiles):
            term = dot(invs[t], held[index, :, span_of(t)], NT)
            total = term if total is None else total + term
        return jnp.broadcast_to(total[0:1] + total[1:2], (8, crow))

    flows = ((sums_k, keys_a, keys_half, keys_b), (sums_v, vals_a, vals_half, vals_b))
    own_sums = [[None] * cuts, [None] * cuts]
    own_masses = None
    for d in range(chips):
        place = (chip + d + 1) % chips
        far = at(head, place * 2 + core)
        arrivals = {}
        for c in range(cuts):
            index = (place * 2 + other) * cuts + c
            for flow, (term, (mine, came, _, _)) in enumerate(
                zip(second_part(place, other, c), flows)
            ):
                mine[index] = term
                arrivals[flow, c] = begin(
                    mine.at[index], came.at[d, c], a_send.at[1 + flow, d, c],
                    a_recv.at[1 + flow, d, c], partner,
                )
        for c in range(cuts):
            mass[place, c] = mass_part(place, other, c)
        mass_arrival = begin(
            mass.at[place], mass_a.at[d], a_send.at[3, d, 0], a_recv.at[3, d, 0], partner
        )
        for c in range(cuts):
            terms = second_part(place, core, c)
            if c == cuts - 1:
                masses = [mass_part(place, core, e) for e in range(cuts)]
                mass_arrival.wait_recv()
                masses = [masses[e] + mass_a[d, e] for e in range(cuts)]
                if d == chips - 1:
                    own_masses = masses
                else:
                    for e in range(cuts):
                        mass_half[d, e] = masses[e]
                    begin(
                        mass_half.at[d], mass_b.at[d], b_send.at[3, d, 0], b_recv.at[3, d, 0], far
                    )
            for flow, (term, (_, came, half, slots)) in enumerate(zip(terms, flows)):
                arrivals[flow, c].wait_recv()
                term = term + came[d, c]
                if d == chips - 1:
                    own_sums[flow][c] = term
                    continue
                half[d, c] = term.astype(half.dtype)
                begin(
                    half.at[d, c], slots.at[d, c], b_send.at[1 + flow, d, c],
                    b_recv.at[1 + flow, d, c], far,
                )

    exact_weighted = dot(exact_prob, values[...].reshape(heads * tok_dev, dim), NN)

    def landed(slots, row, d, c):
        slot = slots.at[d, c]
        remote(slot, slot, b_send.at[row, d, c], b_recv.at[row, d, c], partner).wait_recv()

    for d in range(chips - 1):
        slot = mass_b.at[d]
        remote(slot, slot, b_send.at[3, d, 0], b_recv.at[3, d, 0], partner).wait_recv()
        own_masses = [own_masses[c] + mass_b[d, c] for c in range(cuts)]
    mass_row = jnp.concatenate([m[0:1] for m in own_masses], axis=1)
    log_mass = jnp.log(mass_row)
    eye = lax.broadcasted_iota(jnp.int32, (share, share), 0) == lax.broadcasted_iota(
        jnp.int32, (share, share), 1
    )
    mass_column = jnp.sum(jnp.where(eye, mass_row, 0.0), axis=1, keepdims=True)

    for c in range(cuts):
        for d in range(chips - 1):
            landed(keys_b, 1, d, c)
            own_sums[0][c] = own_sums[0][c] + keys_b[d, c].astype(jnp.float32)
    own_keys = jnp.concatenate(own_sums[0], axis=0)
    cent_in[head] = to_unit(own_keys).reshape(heads, owned, dim)
    cent_sends = []
    for k in range(1, heads):
        to = flipped(head, k)
        cent_sends.append(
            begin(
                cent_in.at[head, to], cent_in.at[heads, k], c_send.at[k], c_recv.at[k],
                at(to, member),
            )
        )

    mean_keys = (own_keys / mass_column).astype(jnp.bfloat16)
    score = dot(query, mean_keys, NT) * scale + log_mass
    usable = picked < 0.5
    score = jnp.where(usable, score, NEGATIVE)
    peak = jnp.maximum(jnp.max(score, axis=1, keepdims=True), exact_peak)
    prob = jnp.where(usable, jnp.exp(score - peak), 0.0).astype(jnp.bfloat16)
    exact_factor = jnp.exp(exact_peak - peak)
    weight_sum = jnp.sum(prob.astype(jnp.float32), axis=1, keepdims=True) + exact_sum * exact_factor
    weight_sum = jnp.maximum(weight_sum, 1e-30)
    log_total = peak + jnp.log(weight_sum)
    row_lanes = lax.broadcasted_iota(jnp.int32, (half_rows, stats.shape[2]), 1)
    row_subs = lax.broadcasted_iota(jnp.int32, (half_rows, stats.shape[2]), 0)
    for side in range(2):
        here = log_total[side * half_rows : (side + 1) * half_rows]
        line = jnp.sum(jnp.where(row_lanes == row_subs, here, 0.0), axis=0, keepdims=True)
        stats[side] = jnp.broadcast_to(line, stats.shape[1:])
    for c in range(cuts):
        for d in range(chips - 1):
            landed(vals_b, 2, d, c)
            own_sums[1][c] = own_sums[1][c] + vals_b[d, c].astype(jnp.float32)
    own_values = jnp.concatenate(own_sums[1], axis=0)
    mean_values = (own_values / mass_column).astype(jnp.bfloat16)
    weighted = dot(prob, mean_values, NN) + exact_weighted * exact_factor
    parts[...] = (weighted / weight_sum).astype(parts.dtype).reshape(parts.shape)

    for d in range(1, members):
        to = (member + d) % members
        side = to % 2
        target = at(head, to)
        begin(stats.at[side], fin_stats.at[d], s_send.at[d], s_recv.at[d], target)
        begin(parts.at[side], fin.at[d], f_send.at[d], f_recv.at[d], target)

    totals, means = [stats[core]], [parts[core].astype(jnp.float32)]
    for d in range(1, members):
        slot = fin_stats.at[d]
        remote(slot, slot, s_send.at[d], s_recv.at[d], partner).wait_recv()
        totals.append(fin_stats[d])
    totals = [
        jnp.sum(jnp.where(row_lanes == row_subs, total[0:1], 0.0), axis=1, keepdims=True)
        for total in totals
    ]
    top = functools.reduce(jnp.maximum, totals)
    factors = [jnp.exp(total - top) for total in totals]
    scale_down = 1.0 / functools.reduce(jnp.add, factors)
    for d in range(1, members):
        slot = fin.at[d]
        remote(slot, slot, f_send.at[d], f_recv.at[d], partner).wait_recv()
        means.append(fin[d].astype(jnp.float32))
    upper = functools.reduce(jnp.add, [mean * factor for mean, factor in zip(means, factors)])
    att[head, core] = (upper * scale_down).astype(jnp.bfloat16)
    near = [(k, c) for k in range(heads) for c in range(2)][1:]
    piece = att.at[head, core]
    for index, (k, c) in enumerate(near):
        target = at(flipped(head, k), chip * 2 + (core + c) % 2)
        begin(piece, piece, o_send.at[index], o_recv.at[index], target)

    for copy in cent_sends:
        copy.wait_recv()
    cent_out[head] = cent_in[head, head]
    for k in range(1, heads):
        source = flipped(head, k)
        cent_out[source] = cent_in[heads, k]

    per_half = half_rows // group

    def place_out(of_head, side):
        att_out[pl.ds(side * per_half, per_half), of_head] = (
            att[of_head, side].astype(jnp.float32).reshape(per_half, group, dim).astype(jnp.bfloat16)
        )

    place_out(head, core)
    for copy in sent[: -len(near)]:
        copy.wait_send()
    for index, (k, c) in enumerate(near):
        source, side = flipped(head, k), (core + c) % 2
        piece = att.at[source, side]
        remote(piece, piece, o_send.at[index], o_recv.at[index], partner).wait_recv()
        place_out(source, side)
    for copy in sent[-len(near) :]:
        copy.wait_send()


def put_out(cent_in, att_in, cent_out, att_out, sem):
    copies = (
        pltpu.make_async_copy(cent_in, cent_out, sem.at[0]),
        pltpu.make_async_copy(att_in, att_out, sem.at[1]),
    )
    for copy in copies:
        copy.start()
    for copy in copies:
        copy.wait()


def body(
    key_cache,
    value_cache,
    init_centroids,
    block_clusters,
    chosen_clusters,
    request_positions,
    queries,
):
    n = lax.axis_size("ctx")
    heads, tok_dev, dim = key_cache.shape
    requests, _, group, _ = queries.shape
    clusters = init_centroids.shape[1]
    members = n // heads
    chips = members // 2
    share = clusters // members
    owned = clusters // n
    cuts = 2 if share % 256 == 0 else 1
    crow = share // cuts
    half_rows = requests * group // 2
    f32, bf16 = jnp.float32, jnp.bfloat16
    vmem, dma = pltpu.VMEM, pltpu.SemaphoreType.DMA
    anywhere = pl.BlockSpec(memory_space=pl.ANY)
    in_vmem = pl.BlockSpec(memory_space=pltpu.VMEM)
    whole = (members * cuts, crow, dim)
    half = (chips, cuts, crow, dim)
    small = (chips, cuts, 8, crow)
    tile = math.gcd(256, tok_dev)
    tiles = tok_dev // tile
    tokens = heads * tok_dev
    results = pl.pallas_call(
        functools.partial(kernel, n, tile),
        out_shape=(
            vmem((heads, owned, dim), f32),
            vmem(queries.shape, bf16),
        ),
        in_specs=[anywhere] * 7,
        out_specs=(in_vmem, in_vmem),
        scratch_shapes=[
            vmem(queries.shape, bf16),
            vmem(chosen_clusters.shape, jnp.int32),
            pltpu.SMEM(block_clusters.shape, jnp.int32),
            pltpu.SMEM(request_positions.shape, jnp.int32),
            vmem((clusters, dim), bf16),
            vmem((heads, tok_dev, dim), bf16),
            vmem((heads * tiles, tile, dim), bf16),
            vmem((heads, tok_dev, dim), bf16),
            vmem(whole, bf16),
            vmem((members * cuts, crow, tokens), bf16),
            vmem((tokens, 2 * dim), bf16),
            vmem((heads * tiles, 8, tile), f32),
            vmem((heads * tiles, 16, tile), bf16),
            vmem(whole, f32),
            vmem(whole, f32),
            vmem(whole, f32),
            vmem(small, f32),
            vmem(half, f32),
            vmem(half, bf16),
            vmem(half, bf16),
            vmem(half, f32),
            vmem(half, f32),
            vmem(small, f32),
            vmem(half, bf16),
            vmem(half, bf16),
            vmem(small, f32),
            vmem(half, bf16),
            vmem(half, bf16),
            vmem(small, f32),
            vmem(whole, bf16),
            vmem((heads + 1, heads, owned, dim), f32),
            vmem((2, 8, 128), f32),
            vmem((2, half_rows, dim), bf16),
            vmem((members, 8, 128), f32),
            vmem((members, half_rows, dim), bf16),
            vmem((heads, 2, half_rows, dim), bf16),
            dma((3,)),
            dma((4,)),
            pltpu.SemaphoreType.REGULAR((2,)),
            dma((heads, tiles)),
            dma((heads, tiles)),
            dma((heads,)),
            dma((heads,)),
            dma((4, chips, cuts)),
            dma((4, chips, cuts)),
            dma((4, chips, cuts)),
            dma((4, chips, cuts)),
            dma((2 * chips, cuts)),
            dma((2 * chips, cuts)),
            dma((heads,)),
            dma((heads,)),
            dma((members,)),
            dma((members,)),
            dma((members,)),
            dma((members,)),
            dma((2 * heads,)),
            dma((2 * heads,)),
        ],
        compiler_params=pltpu.CompilerParams(
            collective_id=0, has_side_effects=True, vmem_limit_bytes=56 * 1024 * 1024
        ),
    )(
        key_cache,
        value_cache,
        init_centroids,
        queries,
        chosen_clusters,
        block_clusters,
        request_positions,
    )
    return tuple(
        pl.pallas_call(
            put_out,
            out_shape=tuple(jax.ShapeDtypeStruct(x.shape, x.dtype) for x in results),
            in_specs=[anywhere, anywhere],
            out_specs=(anywhere, anywhere),
            scratch_shapes=[dma((2,))],
        )(*(pltpu.with_memory_space_constraint(x, pltpu.VMEM) for x in results))
    )


def solution(mesh):
    placed = (
        P(None, ("groups", "ctx"), None),
        P(None, ("groups", "ctx"), None),
        P(),
        P(None, "groups"),
        P("groups", None, None),
        P("groups"),
        P("groups", None, None, None),
    )
    return jax.shard_map(
        body,
        mesh=mesh,
        in_specs=placed,
        out_specs=(P(None, ("groups", "ctx"), None), P("groups", None, None, None)),
        check_vma=False,
    )
```
